32 devices in a mesh: groups: 2 (over y), snap: 4 (over z), slab: 2 (over x), sub: 2 (over core).
Axes of the slice: x: 2, y: 2, z: 4, core: 2. Of those that a mesh axis runs over, the one named last changes fastest.
Arguments:
- fields: float32 [8, 4, 4, 16, 128], P(('groups', 'snap'), None, 'slab', 'sub'), parts along dimension 0, may hold values from -18 to 18
- snap_ids: int32 [8], P(('groups', 'snap')), parts along dimension 0, may hold values from 0 to 63
- snap_weight: float32 [64], replicated, may hold values from 0.5 to 2
- product_terms: int32 [192, 3], replicated, may hold values from 0 to 27, as said below
- mix_weight: float32 [192], replicated, may hold values from -1.5 to 1.5
Outputs:
- whitened: bfloat16 [8, 192, 4, 16, 128], P(('groups', 'snap'), None, 'slab', 'sub'), parts along dimension 0
- r_factor: float32 [384, 192], P('groups'), parts along dimension 0
The draws below stay inside these ranges and needn't reach their ends.
There are 2 independent parts, one for each index of `groups`. The reference program is written for one: setup_inputs(seed, part) draws one part's arguments, and reference() takes and returns one part's arrays. A program takes and returns all parts, laid end to end along the dimension named above; an argument that names none is the same for every part. Nothing has to cross between parts.
Inputs may be any that keep to these rules, and one draw needn't show every extreme that they name: `product_terms`: each row names three different bases, and no two rows are equal.
All inputs are finite; a program needn't handle non-finite values.
Results may differ from the reference program's by a relative error of at most 0.0028.
Values sent between devices are 32-bit elements; how exact they have to be, the bound alone decides.
A program may use at most 64 MiB of HBM per device.

```python
import math
import jax
import jax.numpy as jnp
from jax import lax

NY = 128
NFEAT = 192
NBASE = 28
TABLE = 64
SNAPS = 4
NZ = 4
NX = 16
CELLS = 32768


def draw_fields(key, part):
    shape = (SNAPS, 4, NZ, NX, NY)
    ramp = 1.0 + 2.0 * jnp.arange(SNAPS, dtype=jnp.float32) / max(SNAPS - 1, 1)
    ramp = ramp[:, None, None, None, None]
    values = ramp * jnp.clip(jax.random.normal(key, shape, jnp.float32), -6.0, 6.0)
    return values


def draw_product_terms(key, part):
    count_all = NBASE * (NBASE - 1) * (NBASE - 2)
    codes = jax.random.permutation(key, count_all)[:NFEAT].astype(jnp.int32)
    span_inner = (NBASE - 1) * (NBASE - 2)
    first_index = codes // span_inner
    remain = codes % span_inner
    second_raw = remain // (NBASE - 2)
    third_raw = remain % (NBASE - 2)
    second_index = second_raw + (second_raw >= first_index).astype(jnp.int32)
    lower_index = jnp.minimum(first_index, second_index)
    upper_index = jnp.maximum(first_index, second_index)
    third_index = third_raw + (third_raw >= lower_index).astype(jnp.int32)
    third_index = third_index + (third_index >= upper_index).astype(jnp.int32)
    return jnp.stack([first_index, second_index, third_index], axis=1).astype(jnp.int32)


def with_ends(drawn, key, low, top_value):
    longest = drawn.shape.index(max(drawn.shape))
    spots = []
    for shift in (0, 1):
        where = [jax.random.randint(jax.random.fold_in(key, axis), (), 0, length) for axis, length in enumerate(drawn.shape)]
        where[longest] = (where[longest] + shift) % drawn.shape[longest]
        spots.append(tuple(where))
    return drawn.at[spots[0]].set(low).at[spots[1]].set(top_value)


def setup_inputs(seed: int = 0, part: int = 0) -> dict:
    keys = jax.random.split(jax.random.key(seed), 6)
    part_keys = jax.random.split(jax.random.fold_in(keys[5], part), 6)
    return {
        "fields": draw_fields(jax.random.fold_in(jax.random.fold_in(keys[5], part), 71), part),
        "snap_ids": with_ends(jax.random.randint(part_keys[1], (SNAPS,), 0, TABLE), jax.random.fold_in(part_keys[1], 1), 0, TABLE - 1).astype(jnp.int32),
        "snap_weight": jnp.clip(jnp.exp(jax.random.uniform(keys[2], (TABLE,), jnp.float32, math.log(0.5), math.log(2.0))), 0.5, 2.0),
        "product_terms": draw_product_terms(jax.random.fold_in(keys[5], 71), part),
        "mix_weight": jnp.clip(jax.random.uniform(keys[4], (NFEAT,), jnp.float32, -1.5, 1.5), -1.5, 1.5),
    }


ridge_value = 0.05

def stencil_pair(values, along):
    ahead_one = jnp.roll(values, -1, along)
    behind_one = jnp.roll(values, 1, along)
    ahead_two = jnp.roll(values, -2, along)
    behind_two = jnp.roll(values, 2, along)
    first_deriv = (8.0 * (ahead_one - behind_one) - (ahead_two - behind_two)) / 12.0
    second_deriv = (16.0 * (ahead_one + behind_one) - (ahead_two + behind_two) - 30.0 * values) / 12.0
    return (first_deriv, second_deriv)

def snapshot_features(field_block, snap_scale, product_terms, mix_weight):
    z_first, z_second = stencil_pair(field_block, 1)
    x_first, x_second = stencil_pair(field_block, 2)
    y_first, y_second = stencil_pair(field_block, 3)
    stacked = jnp.stack([field_block, z_first, x_first, y_first, z_second, x_second, y_second], axis=1)
    bases = stacked.reshape(NBASE, -1)
    left_term = bases[product_terms[:, 0]]
    middle = bases[product_terms[:, 1]]
    right_term = bases[product_terms[:, 2]]
    return snap_scale * left_term * (middle + mix_weight[:, None] * right_term)

def reference(fields, snap_ids, snap_weight, product_terms, mix_weight):
    scales = snap_weight[snap_ids.astype(jnp.int32)]

    def accumulate(total_gram, snapshot):
        field_block, snap_scale = snapshot
        features = snapshot_features(field_block, snap_scale, product_terms, mix_weight)
        product = lax.dot_general(features, features, (((1,), (1,)), ((), ())), precision=lax.Precision.HIGHEST)
        return (total_gram + product, None)
    total_gram, _ = lax.scan(accumulate, jnp.zeros((NFEAT, NFEAT), jnp.float32), (fields, scales))
    gram = total_gram / CELLS + ridge_value * jnp.eye(NFEAT, dtype=jnp.float32)
    r_factor = jnp.linalg.cholesky(gram).T

    def whiten(snapshot):
        field_block, snap_scale = snapshot
        features = snapshot_features(field_block, snap_scale, product_terms, mix_weight)
        solved = jax.scipy.linalg.solve_triangular(r_factor, features, trans=1, lower=False)
        return solved.reshape(NFEAT, NZ, NX, NY).astype(jnp.bfloat16)
    whitened = lax.map(whiten, (fields, scales))
    return (whitened, r_factor)
```

```python
import functools

import jax
import jax.numpy as jnp
from jax import lax
from jax.experimental import pallas as pl
from jax.experimental.pallas import tpu as pltpu
from jax.sharding import PartitionSpec as P

ridge_value = 0.05
panel_rows = 32
HIGHEST = lax.Precision.HIGHEST
MESH = pl.DeviceIdType.MESH


def split(values, count):
    parts = []
    for _ in range(count):
        part = values.astype(jnp.bfloat16)
        parts.append(part)
        values = values - part.astype(jnp.float32)
    return parts


def row_of(tile, place):
    return jnp.broadcast_to(tile[place : place + 1, :], tile.shape)


def eliminate_group(groups, first, place):
    line = lax.broadcasted_iota(jnp.int32, (8, 128), 0)
    lane_tile, lane = place // 128, place % 128
    later = range(first, len(groups))
    spread = {
        (r, c): jnp.broadcast_to(
            groups[r][lane_tile][:, lane + c : lane + c + 1], (8, 128)
        )
        for r in later
        for c in range(8)
    }
    pivots = jnp.ones((8, 128), jnp.float32)
    factors = []
    for j in range(8):
        pivot = row_of(spread[first, j], j)
        pivots = jnp.where(line == j, pivot, pivots)
        inverse = 1.0 / pivot
        scaled = {r: spread[r, j] * inverse for r in later}
        scaled[first] = jnp.where(line > j, scaled[first], 0.0)
        factors.append(scaled)
        for c in range(j + 1, 8):
            head = row_of(spread[first, c], j)
            for r in later:
                spread[r, c] = spread[r, c] - scaled[r] * head
    for t in range(len(groups[first])):
        tile = groups[first][t]
        for j in range(8):
            head = row_of(tile, j)
            if j < 7:
                tile = tile - factors[j][first] * head
            for r in later:
                if r > first:
                    groups[r][t] = groups[r][t] - factors[j][r] * head
        groups[first][t] = tile
    return 1.0 / jnp.sqrt(pivots)


def eliminate(work, order):
    half = work.shape[1] // 2
    for start in range(0, order, panel_rows):
        stop = start + panel_rows
        low = start // 128 * 128
        high = half + (stop + 127) // 128 * 128
        tiles = (high - low) // 128
        groups = [
            [work[r : r + 8, low + 128 * t : low + 128 * t + 128] for t in range(tiles)]
            for r in range(start, stop, 8)
        ]
        scales = [
            eliminate_group(groups, g, start + 8 * g - low) for g in range(panel_rows // 8)
        ]
        rows = [
            jnp.concatenate([tile * scale for tile in group], axis=1)
            for group, scale in zip(groups, scales)
        ]
        panel = jnp.concatenate(rows, axis=0)
        work[start:stop, low:high] = panel
        if stop < order:
            sides = panel[:, : half - low].T[stop - low : order - low, :]
            a, b, c = split(sides, 3)
            d, e, f = split(panel, 3)
            left = jnp.concatenate([a, a, b, b, a, c], axis=1)
            right = jnp.concatenate([d, e, d, e, f, d], axis=0)
            work[stop:order, low:high] = work[stop:order, low:high] - jnp.dot(
                left, right, preferred_element_type=jnp.float32
            )


def whiten_kernel(
    cells_total, packed_ref, feature_ref, white_ref, factor_ref, work, spread
):
    order = factor_ref.shape[0]
    middle = packed_ref.shape[0]
    half = work.shape[1] // 2
    rows = lax.broadcasted_iota(jnp.int32, (order, order), 0)
    columns = lax.broadcasted_iota(jnp.int32, (order, order), 1)
    row = lax.broadcasted_iota(jnp.int32, (middle, 128), 0)
    lane = lax.broadcasted_iota(jnp.int32, (middle, 128), 1)
    left = packed_ref[:, :128]
    turned = jnp.concatenate([left, jnp.zeros((128 - middle, 128), jnp.float32)], axis=0).T
    turned = turned[:middle, :]
    work[:middle, :128] = jnp.where((lane >= row) | (lane >= middle), left, turned)
    work[:middle, 128:half] = jnp.where(lane + 128 < order, packed_ref[:, 128:], 0.0)
    corner = packed_ref[:, order : order + 1]
    lower = jnp.where(lane < row, left, jnp.where(lane > row, turned, corner))
    lower = jnp.where(lane < middle, lower, 0.0)
    lower = jnp.concatenate([lower, jnp.zeros((middle, half - 128), jnp.float32)], axis=1)
    work[middle:, :half] = pltpu.roll(lower, middle, 1)
    long_rows = lax.broadcasted_iota(jnp.int32, (order, half), 0)
    long_columns = lax.broadcasted_iota(jnp.int32, (order, half), 1)
    identity = (long_rows == long_columns).astype(jnp.float32)
    work[:, half:] = identity
    work[:, :half] = work[:, :half] * (1.0 / cells_total) + ridge_value * identity
    eliminate(work, order)
    factor_ref[...] = jnp.where(columns >= rows, work[:, :order], 0.0)
    inverse = jnp.where(columns <= rows, work[:, half : half + order], 0.0)
    upper, lower = split(inverse, 2)
    tiles = feature_ref.shape[1] // 128
    for tile in range(0, tiles, 2):
        first, second = split(feature_ref[:, tile * 128 : tile * 128 + 256], 2)
        solved = (
            jnp.dot(upper, first, preferred_element_type=jnp.float32)
            + jnp.dot(upper, second, preferred_element_type=jnp.float32)
            + jnp.dot(lower, first, preferred_element_type=jnp.float32)
        )
        spread[pl.ds(tile, order, stride=tiles), :] = solved[:, :128]
        spread[pl.ds(tile + 1, order, stride=tiles), :] = solved[:, 128:]
    white_ref[...] = spread[...].reshape(white_ref.shape).astype(white_ref.dtype)


def plane_device(place, subs):
    return {"slab": lax.div(place, subs), "sub": lax.rem(place, subs)}


def gram_kernel(
    counts,
    fields_in,
    ids_in,
    weight_in,
    terms_in,
    mix_in,
    packed_ref,
    feature_ref,
    fields_ref,
    ids_ref,
    weight_ref,
    terms_ref,
    mix_ref,
    load_done,
    gram_wide,
    halo_z,
    halo_x,
    natural,
    partial,
    landed,
    snaps_sum,
    total,
    halo_send,
    halo_recv,
    plane_send,
    plane_recv,
    snap_send,
    snap_recv,
    gather_send,
    gather_recv,
):
    slabs, subs, snaps = counts
    plane = slabs * subs
    slab, sub, snap = lax.axis_index("slab"), lax.axis_index("sub"), lax.axis_index("snap")
    me = slab * subs + sub
    plane_peers = [plane_device(lax.rem(me + k, plane), subs) for k in range(1, plane)]
    snap_peers = [{"snap": lax.rem(snap + k, snaps)} for k in range(1, snaps)]

    loads = [
        pltpu.make_async_copy(source, target, load_done.at[k])
        for k, (source, target) in enumerate(
            (
                (fields_in, fields_ref),
                (terms_in, terms_ref),
                (mix_in, mix_ref),
                (weight_in, weight_ref),
                (ids_in, ids_ref),
            )
        )
    ]
    for load in loads:
        load.start()
    barrier = pltpu.get_barrier_semaphore()
    for peer in plane_peers + snap_peers:
        pl.semaphore_signal(barrier, inc=1, device_id=peer, device_id_type=MESH)
    for load in loads:
        load.wait()
    features = terms_ref.shape[1]
    field_count, layers, columns, width = fields_ref.shape[1:]
    cells_rows = layers * columns
    square_rows = lax.broadcasted_iota(jnp.int32, (features, features), 0)
    square_columns = lax.broadcasted_iota(jnp.int32, (features, features), 1)

    def upright(row):
        return jnp.sum(jnp.where(square_rows == square_columns, row, 0.0), axis=1, keepdims=True)

    slot = lax.broadcasted_iota(jnp.int32, (features, 96), 1)
    base_of = lax.rem(slot, 32).astype(jnp.float32)
    chosen = [
        (upright(terms_ref[k : k + 1, :].astype(jnp.float32)) == base_of)
        .astype(jnp.float32)
        .astype(jnp.bfloat16)
        for k in range(3)
    ]
    choose = jnp.concatenate(chosen, axis=0)
    mix = upright(mix_ref[...])
    table = lax.broadcasted_iota(jnp.int32, weight_ref.shape, 1)
    scale = jnp.sum(
        jnp.where(table == ids_ref[...], weight_ref[...], 0.0), axis=1, keepdims=True
    )
    natural[28 * cells_rows :, :] = jnp.zeros((4 * cells_rows, width), jnp.float32)

    def put(field, kind, layer, tile):
        start = (field * 7 + kind) * cells_rows + layer * columns
        natural[start : start + columns, :] = tile

    def pair(center, ahead_one, behind_one, ahead_two, behind_two):
        first = 8.0 * (ahead_one - behind_one) - (ahead_two - behind_two)
        second = 16.0 * (ahead_one + behind_one) - (ahead_two + behind_two) - 30.0 * center
        return first * (1.0 / 12.0), second * (1.0 / 12.0)

    for f in range(field_count):
        for z in range(layers):
            tile = fields_ref[0, f, z]
            put(f, 0, z, tile)
            y_shifts = [pltpu.roll(tile, s % width, 1) for s in (-1, 1, -2, 2)]
            first, second = pair(tile, *y_shifts)
            put(f, 3, z, first)
            put(f, 6, z, second)

    pl.semaphore_wait(barrier, len(plane_peers) + len(snap_peers))

    copies = []
    for axis, index, count, halo, base in (
        ("slab", slab, slabs, halo_z, 0),
        ("sub", sub, subs, halo_x, 2),
    ):
        for side, move in ((0, 1), (1, count - 1))[: 1 if count == 2 else 2]:
            copy = pltpu.make_async_remote_copy(
                src_ref=fields_ref.at[0],
                dst_ref=halo.at[side],
                send_sem=halo_send.at[base + side],
                recv_sem=halo_recv.at[base + side],
                device_id={axis: lax.rem(index + move, count)},
                device_id_type=MESH,
            )
            copy.start()
            copies.append(copy)

    for copy in copies:
        copy.wait()

    z_low, z_high = 0, 0 if slabs == 2 else 1
    x_low, x_high = 0, 0 if subs == 2 else 1
    line = lax.broadcasted_iota(jnp.int32, (columns, width), 0)
    for f in range(field_count):
        column = [halo_z[z_low, f, z] for z in range(layers)]
        column += [fields_ref[0, f, z] for z in range(layers)]
        column += [halo_z[z_high, f, z] for z in range(layers)]
        for z in range(layers):
            tile = column[layers + z]
            at = layers + z
            first, second = pair(
                tile, column[at + 1], column[at - 1], column[at + 2], column[at - 2]
            )
            put(f, 1, z, first)
            put(f, 4, z, second)
            low, high = halo_x[x_low, f, z], halo_x[x_high, f, z]
            shifts = []
            for s in (-1, 1, -2, 2):
                turned = pltpu.roll(tile, s % columns, 0)
                other = pltpu.roll(high if s < 0 else low, s % columns, 0)
                inside = line < columns + s if s < 0 else line >= s
                shifts.append(jnp.where(inside, turned, other))
            first, second = pair(tile, *shifts)
            put(f, 2, z, first)
            put(f, 5, z, second)

    for start in range(0, cells_rows, 2):
        pieces = []
        for at in (start, start + 1):
            whole = natural[pl.ds(at, 32, stride=cells_rows), :]
            upper = whole.astype(jnp.bfloat16)
            rest = whole - upper.astype(jnp.float32)
            centre = rest.astype(jnp.bfloat16)
            lower = (rest - centre.astype(jnp.float32)).astype(jnp.bfloat16)
            pieces.append(jnp.concatenate([upper, centre, lower], axis=0))
        picked = jnp.dot(
            choose, jnp.concatenate(pieces, axis=1), preferred_element_type=jnp.float32
        )
        left, middle = picked[:features], picked[features : 2 * features]
        right = picked[2 * features :]
        feature_ref[:, start * width : (start + 2) * width] = (
            scale * left * (middle + mix * right)
        )

    everything = feature_ref[...]
    wide = gram_wide.shape[1]
    gram_wide[:, :features] = lax.dot_general(
        everything,
        everything,
        (((1,), (1,)), ((), ())),
        precision=HIGHEST,
        preferred_element_type=jnp.float32,
    )
    half = features // 2
    above = gram_wide[:half, :]
    below = gram_wide[half:, :]
    row = lax.broadcasted_iota(jnp.int32, (half, wide), 0)
    lane = lax.broadcasted_iota(jnp.int32, (half, wide), 1)
    corner = jnp.sum(jnp.where(lane == row + half, below, 0.0), axis=1, keepdims=True)
    packed = jnp.where(
        lane < half,
        jnp.where(lane >= row, above, pltpu.roll(below, wide - half, 1)),
        jnp.where(lane < features, above, corner),
    )
    rows = half // plane
    for k in range(plane):
        partial[k] = packed[k * rows : (k + 1) * rows, :]

    copies = []
    for k in range(1, plane):
        copy = pltpu.make_async_remote_copy(
            src_ref=partial.at[lax.rem(me + k, plane)],
            dst_ref=landed.at[k - 1],
            send_sem=plane_send.at[k - 1],
            recv_sem=plane_recv.at[k - 1],
            device_id=plane_peers[k - 1],
            device_id_type=MESH,
        )
        copy.start()
        copies.append(copy)
    block = partial[me]
    for k in range(1, plane):
        copies[k - 1].wait()
        block = block + landed[k - 1]
    snaps_sum[snap] = block

    copies = []
    for k in range(1, snaps):
        copy = pltpu.make_async_remote_copy(
            src_ref=snaps_sum.at[snap],
            dst_ref=snaps_sum.at[snap],
            send_sem=snap_send.at[k - 1],
            recv_sem=snap_recv.at[k - 1],
            device_id=snap_peers[k - 1],
            device_id_type=MESH,
        )
        copy.start()
        copies.append(copy)
    for copy in copies:
        copy.wait()
    block = snaps_sum[0]
    for k in range(1, snaps):
        block = block + snaps_sum[k]
    total[me] = block

    copies = []
    for k in range(1, plane):
        copy = pltpu.make_async_remote_copy(
            src_ref=total.at[me],
            dst_ref=total.at[me],
            send_sem=gather_send.at[k - 1],
            recv_sem=gather_recv.at[k - 1],
            device_id=plane_peers[k - 1],
            device_id_type=MESH,
        )
        copy.start()
        copies.append(copy)
    for copy in copies:
        copy.wait()
    for k in range(plane):
        packed_ref[k * rows : (k + 1) * rows, :] = total[k]


def local(fields, snap_ids, snap_weight, product_terms, mix_weight):
    counts = tuple(lax.axis_size(axis) for axis in ("slab", "sub", "snap"))
    slabs, subs, snaps = counts
    plane = slabs * subs
    field_count, layers, columns, width = fields.shape[1:]
    features = product_terms.shape[0]
    cells = layers * columns * width
    half = features // 2
    rows = half // plane
    wide = features // 128 * 128 + 128
    f32 = jnp.float32
    in_vmem = pl.BlockSpec(memory_space=pltpu.VMEM)
    anywhere = pl.BlockSpec(memory_space=pl.ANY)
    total_gram, values = pl.pallas_call(
        functools.partial(gram_kernel, counts),
        out_shape=(
            pltpu.VMEM((half, wide), f32),
            pltpu.VMEM((features, cells), f32),
        ),
        in_specs=[pl.BlockSpec(memory_space=pltpu.HBM)] * 5,
        out_specs=(in_vmem, in_vmem),
        scratch_shapes=[
            pltpu.VMEM(fields.shape, f32),
            pltpu.VMEM((1, 1), jnp.int32),
            pltpu.VMEM((1, snap_weight.shape[0]), f32),
            pltpu.VMEM((3, features), jnp.int32),
            pltpu.VMEM((1, features), f32),
            pltpu.SemaphoreType.DMA((5,)),
            pltpu.VMEM((features, wide), f32),
            pltpu.VMEM((2,) + fields.shape[1:], f32),
            pltpu.VMEM((2,) + fields.shape[1:], f32),
            pltpu.VMEM((32 * layers * columns, width), f32),
            pltpu.VMEM((plane, rows, wide), f32),
            pltpu.VMEM((plane - 1, rows, wide), f32),
            pltpu.VMEM((snaps, rows, wide), f32),
            pltpu.VMEM((plane, rows, wide), f32),
            pltpu.SemaphoreType.DMA((4,)),
            pltpu.SemaphoreType.DMA((4,)),
            pltpu.SemaphoreType.DMA((plane - 1,)),
            pltpu.SemaphoreType.DMA((plane - 1,)),
            pltpu.SemaphoreType.DMA((snaps - 1,)),
            pltpu.SemaphoreType.DMA((snaps - 1,)),
            pltpu.SemaphoreType.DMA((plane - 1,)),
            pltpu.SemaphoreType.DMA((plane - 1,)),
        ],
        compiler_params=pltpu.CompilerParams(collective_id=0, has_side_effects=True),
    )(fields, snap_ids.reshape(1, 1), snap_weight.reshape(1, -1), product_terms.T, mix_weight.reshape(1, -1))
    whitened, r_factor = pl.pallas_call(
        functools.partial(whiten_kernel, float(snaps * plane * cells)),
        out_shape=(
            jax.ShapeDtypeStruct((1, features, layers, columns, width), jnp.bfloat16),
            jax.ShapeDtypeStruct((features, features), f32),
        ),
        in_specs=[in_vmem, in_vmem],
        out_specs=(in_vmem, in_vmem),
        scratch_shapes=[
            pltpu.VMEM((features, 2 * wide), f32),
            pltpu.VMEM((features * (cells // 128), 128), f32),
        ],
        compiler_params=pltpu.CompilerParams(vmem_limit_bytes=24 * 1024 * 1024),
    )(
        pltpu.with_memory_space_constraint(total_gram, pltpu.VMEM),
        pltpu.with_memory_space_constraint(values, pltpu.VMEM),
    )
    return (whitened, r_factor)


def solution(mesh):
    return jax.shard_map(
        local,
        mesh=mesh,
        in_specs=(
            P(("groups", "snap"), None, "slab", "sub", None),
            P(("groups", "snap")),
            P(),
            P(),
            P(),
        ),
        out_specs=(P(("groups", "snap"), None, "slab", "sub", None), P("groups", None)),
        check_vma=False,
    )
```

```python
import functools

import jax
import jax.numpy as jnp
from jax import lax
from jax.experimental import pallas as pl
from jax.experimental.pallas import tpu as pltpu
from jax.sharding import PartitionSpec as P

ridge_value = 0.05
panel_rows = 64
feature_cut = 64
HIGHEST = lax.Precision.HIGHEST
MESH = pl.DeviceIdType.MESH


def split(values, count):
    parts = []
    for _ in range(count):
        part = values.astype(jnp.bfloat16)
        parts.append(part)
        values = values - part.astype(jnp.float32)
    return parts


def row_of(tile, place):
    return jnp.broadcast_to(tile[place : place + 1, :], tile.shape)


def eliminate_group(groups, first, place):
    line = lax.broadcasted_iota(jnp.int32, (8, 128), 0)
    lane_tile, lane = place // 128, place % 128
    later = range(first, len(groups))
    spread = {
        (r, c): jnp.broadcast_to(
            groups[r][lane_tile][:, lane + c : lane + c + 1], (8, 128)
        )
        for r in later
        for c in range(8)
    }
    pivots = jnp.ones((8, 128), jnp.float32)
    factors = []
    for j in range(8):
        pivot = row_of(spread[first, j], j)
        pivots = jnp.where(line == j, pivot, pivots)
        inverse = 1.0 / pivot
        scaled = {r: spread[r, j] * inverse for r in later}
        scaled[first] = jnp.where(line > j, scaled[first], 0.0)
        factors.append(scaled)
        for c in range(j + 1, 8):
            head = row_of(spread[first, c], j)
            for r in later:
                spread[r, c] = spread[r, c] - scaled[r] * head
    for t in range(len(groups[first])):
        tile = groups[first][t]
        for j in range(8):
            head = row_of(tile, j)
            if j < 7:
                tile = tile - factors[j][first] * head
            for r in later:
                if r > first:
                    groups[r][t] = groups[r][t] - factors[j][r] * head
        groups[first][t] = tile
    return 1.0 / jnp.sqrt(pivots)


def eliminate(work, order):
    half = work.shape[1] // 2
    for start in range(0, order, panel_rows):
        stop = start + panel_rows
        low = start // 128 * 128
        high = half + (stop + 127) // 128 * 128
        tiles = (high - low) // 128
        groups = [
            [work[r : r + 8, low + 128 * t : low + 128 * t + 128] for t in range(tiles)]
            for r in range(start, stop, 8)
        ]
        scales = [
            eliminate_group(groups, g, start + 8 * g - low) for g in range(panel_rows // 8)
        ]
        rows = [
            jnp.concatenate([tile * scale for tile in group], axis=1)
            for group, scale in zip(groups, scales)
        ]
        panel = jnp.concatenate(rows, axis=0)
        work[start:stop, low:high] = panel
        if stop < order:
            sides = panel[:, : half - low].T[stop - low : order - low, :]
            a, b, c = split(sides, 3)
            d, e, f = split(panel, 3)
            left = jnp.concatenate([a, a, b, b, a, c], axis=1)
            right = jnp.concatenate([d, e, d, e, f, d], axis=0)
            work[stop:order, low:high] = work[stop:order, low:high] - jnp.dot(
                left, right, preferred_element_type=jnp.float32
            )


def load_packed(packed_ref, work, order):
    middle = packed_ref.shape[0]
    half = work.shape[1] // 2
    row = lax.broadcasted_iota(jnp.int32, (middle, 128), 0)
    lane = lax.broadcasted_iota(jnp.int32, (middle, 128), 1)
    left = packed_ref[:, :128]
    turned = jnp.concatenate([left, jnp.zeros((128 - middle, 128), jnp.float32)], axis=0).T
    turned = turned[:middle, :]
    work[:middle, :128] = jnp.where((lane >= row) | (lane >= middle), left, turned)
    work[:middle, 128:half] = jnp.where(lane + 128 < order, packed_ref[:, 128:], 0.0)
    corner = packed_ref[:, order : order + 1]
    lower = jnp.where(lane < row, left, jnp.where(lane > row, turned, corner))
    lower = jnp.where(lane < middle, lower, 0.0)
    lower = jnp.concatenate([lower, jnp.zeros((middle, half - 128), jnp.float32)], axis=1)
    work[middle:, :half] = pltpu.roll(lower, middle, 1)


def load_chunks(chunks_ref, work, order):
    line = lax.broadcasted_iota(jnp.int32, (32, 128), 1)

    def spare(tile):
        near = jnp.where(line < 64, tile, 0.0)
        far = pltpu.roll(jnp.where(line >= 64, tile, 0.0), 64, 1)
        return jnp.concatenate([near, far], axis=0)

    head, tail = chunks_ref[0], chunks_ref[1]
    work[:64, :128] = head[:64]
    work[:64, 128:256] = spare(head[64:])
    middle = jnp.concatenate([tail[:64], jnp.zeros((64, 128), jnp.float32)], axis=1)
    work[64:128, :256] = pltpu.roll(middle, 64, 1)
    work[128:192, :128] = jnp.zeros((64, 128), jnp.float32)
    work[128:192, 128:256] = spare(tail[64:])


def whiten_kernel(
    cells_total, load_gram, gram_ref, feature_ref, white_ref, factor_ref, work, spread
):
    order = factor_ref.shape[0]
    half = work.shape[1] // 2
    rows = lax.broadcasted_iota(jnp.int32, (order, order), 0)
    columns = lax.broadcasted_iota(jnp.int32, (order, order), 1)
    load_gram(gram_ref, work, order)
    long_rows = lax.broadcasted_iota(jnp.int32, (order, half), 0)
    long_columns = lax.broadcasted_iota(jnp.int32, (order, half), 1)
    identity = (long_rows == long_columns).astype(jnp.float32)
    work[:, half:] = identity
    work[:, :half] = work[:, :half] * (1.0 / cells_total) + ridge_value * identity
    eliminate(work, order)
    factor_ref[...] = jnp.where(columns >= rows, work[:, :order], 0.0)
    inverse = jnp.where(columns <= rows, work[:, half : half + order], 0.0)
    upper, lower = split(inverse, 2)
    cut = feature_cut
    rest = order - cut
    weights = jnp.concatenate([upper[:, cut:], upper[:, cut:], upper[:, :cut], upper[:, :cut]], axis=1)
    small = jnp.concatenate([lower[:, cut:], lower[:, :cut]], axis=1)
    tiles = feature_ref.shape[1] // 128
    for tile in range(0, tiles, 2):
        both = feature_ref[:, tile * 128 : tile * 128 + 256]
        high = jnp.concatenate([both[:rest], both[2 * rest : 2 * rest + cut]], axis=0)
        solved = jnp.dot(weights, both, preferred_element_type=jnp.float32) + jnp.dot(
            small, high, preferred_element_type=jnp.float32
        )
        spread[pl.ds(tile, order, stride=tiles), :] = solved[:, :128]
        spread[pl.ds(tile + 1, order, stride=tiles), :] = solved[:, 128:]
    white_ref[...] = spread[...].reshape(white_ref.shape).astype(white_ref.dtype)


def plane_device(place, subs):
    return {"slab": lax.div(place, subs), "sub": lax.rem(place, subs)}


def store_features(feature_ref, values, lanes):
    cut, rest = feature_cut, values.shape[0] - feature_cut
    upper, lower = split(values, 2)
    feature_ref[:rest, lanes] = upper[cut:]
    feature_ref[rest : 2 * rest, lanes] = lower[cut:]
    feature_ref[2 * rest : 2 * rest + cut, lanes] = upper[:cut]
    feature_ref[2 * rest + cut :, lanes] = lower[:cut]


def pair(center, ahead_one, behind_one, ahead_two, behind_two):
    first = 8.0 * (ahead_one - behind_one) - (ahead_two - behind_two)
    second = 16.0 * (ahead_one + behind_one) - (ahead_two + behind_two) - 30.0 * center
    return first * (1.0 / 12.0), second * (1.0 / 12.0)


def selection(features, terms_ref, mix_ref):
    square_rows = lax.broadcasted_iota(jnp.int32, (features, features), 0)
    square_columns = lax.broadcasted_iota(jnp.int32, (features, features), 1)

    def upright(row):
        return jnp.sum(jnp.where(square_rows == square_columns, row, 0.0), axis=1, keepdims=True)

    slot = lax.broadcasted_iota(jnp.int32, (features, 96), 1)
    base_of = lax.rem(slot, 32).astype(jnp.float32)
    chosen = [
        (upright(terms_ref[k : k + 1, :].astype(jnp.float32)) == base_of)
        .astype(jnp.float32)
        .astype(jnp.bfloat16)
        for k in range(3)
    ]
    return jnp.concatenate(chosen, axis=0), upright(mix_ref[...])


def picked_products(natural, start, choose, scale, mix):
    features = choose.shape[0] // 3
    cells_rows = natural.shape[0] // 32
    pieces = []
    for at in (start, start + 1):
        pieces.append(
            jnp.concatenate(split(natural[pl.ds(at, 32, stride=cells_rows), :], 3), axis=0)
        )
    picked = jnp.dot(
        choose, jnp.concatenate(pieces, axis=1), preferred_element_type=jnp.float32
    )
    left, middle = picked[:features], picked[features : 2 * features]
    return scale * left * (middle + mix * picked[2 * features :])


def products(left, right):
    return lax.dot_general(
        left, right, (((1,), (1,)), ((), ())), preferred_element_type=jnp.float32
    )


def twin_kernel(
    snaps,
    fields_in,
    ids_in,
    weight_in,
    terms_in,
    mix_in,
    chunks_ref,
    feature_ref,
    blocks,
    ids_ref,
    weight_ref,
    terms_ref,
    mix_ref,
    load_done,
    other_feature,
    natural,
    other_natural,
    partial,
    landed,
    snaps_sum,
    total,
    halo_send,
    halo_recv,
    core_send,
    core_recv,
    snap_send,
    snap_recv,
    gather_send,
    gather_recv,
):
    slab, sub, snap = lax.axis_index("slab"), lax.axis_index("sub"), lax.axis_index("snap")
    twin = {"sub": 1 - sub}
    across = {"slab": 1 - slab}
    corner = {"slab": 1 - slab, "sub": 1 - sub}
    snap_peers = [{"snap": lax.rem(snap + k, snaps)} for k in range(1, snaps)]
    barrier = pltpu.get_barrier_semaphore()
    for peer in [across, corner, twin] + snap_peers:
        pl.semaphore_signal(barrier, inc=1, device_id=peer, device_id_type=MESH)
    loads = [
        pltpu.make_async_copy(source, target, load_done.at[k])
        for k, (source, target) in enumerate(
            (
                (fields_in, blocks.at[pl.ds(0, 1)]),
                (terms_in, terms_ref),
                (mix_in, mix_ref),
                (weight_in, weight_ref),
                (ids_in, ids_ref),
            )
        )
    ]
    for load in loads:
        load.start()
    loads[0].wait()
    pl.semaphore_wait(barrier, 3 + len(snap_peers))
    halos = []
    for slot, peer in ((1, across), (3, corner), (2, twin)):
        copy = pltpu.make_async_remote_copy(
            src_ref=blocks.at[0],
            dst_ref=blocks.at[slot],
            send_sem=halo_send.at[slot - 1],
            recv_sem=halo_recv.at[slot - 1],
            device_id=peer,
            device_id_type=MESH,
        )
        copy.start()
        halos.append(copy)
    for load in loads[1:]:
        load.wait()
    features = terms_ref.shape[1]
    field_count, layers, columns, width = blocks.shape[1:]
    cells_rows = layers * columns
    choose, mix = selection(features, terms_ref, mix_ref)
    table = lax.broadcasted_iota(jnp.int32, weight_ref.shape, 1)
    scale = jnp.sum(
        jnp.where(table == ids_ref[...], weight_ref[...], 0.0), axis=1, keepdims=True
    )
    line = lax.broadcasted_iota(jnp.int32, (columns, width), 0)

    def put(target, field, kind, layer, tile):
        start = (field * 7 + kind) * cells_rows + layer * columns
        target[start : start + columns, :] = tile

    def along_y(target, block):
        target[28 * cells_rows :, :] = jnp.zeros((4 * cells_rows, width), jnp.float32)
        for f in range(field_count):
            for z in range(layers):
                tile = blocks[block, f, z]
                put(target, f, 0, z, tile)
                first, second = pair(tile, *[pltpu.roll(tile, s % width, 1) for s in (-1, 1, -2, 2)])
                put(target, f, 3, z, first)
                put(target, f, 6, z, second)

    def along_x(target, block, beside):
        for f in range(field_count):
            for z in range(layers):
                tile, other = blocks[block, f, z], blocks[beside, f, z]
                shifts = []
                for s in (-1, 1, -2, 2):
                    inside = line < columns + s if s < 0 else line >= s
                    shifts.append(
                        jnp.where(
                            inside,
                            pltpu.roll(tile, s % columns, 0),
                            pltpu.roll(other, s % columns, 0),
                        )
                    )
                first, second = pair(tile, *shifts)
                put(target, f, 2, z, first)
                put(target, f, 5, z, second)

    def along_z(target, block, beside):
        for f in range(field_count):
            column = [blocks[beside, f, z] for z in range(layers)]
            column = column + [blocks[block, f, z] for z in range(layers)] + column
            for z in range(layers):
                at = layers + z
                first, second = pair(
                    column[at], column[at + 1], column[at - 1], column[at + 2], column[at - 2]
                )
                put(target, f, 1, z, first)
                put(target, f, 4, z, second)

    along_y(natural, 0)
    halos[2].wait()
    along_x(natural, 0, 2)
    halos[0].wait()
    along_z(natural, 0, 1)
    for start in range(0, cells_rows, 2):
        values = picked_products(natural, start, choose, scale, mix)
        store_features(feature_ref, values, slice(start * width, (start + 2) * width))
    along_y(other_natural, 1)
    along_z(other_natural, 1, 0)
    halos[1].wait()
    along_x(other_natural, 1, 3)
    for start in range(0, cells_rows, 2):
        values = picked_products(other_natural, start, choose, scale, mix)
        store_features(other_feature, values, slice(start * width, (start + 2) * width))

    cut, rest = feature_cut, features - feature_cut

    def folded(left, right):
        parts = []
        for values in (feature_ref, other_feature):
            both = products(values[left, :], values[right, :])
            high, low = both.shape[0] // 2, both.shape[1] // 2
            both = both[:high] + both[high:]
            parts.append(both[:, :low] + both[:, low:])
        return parts[0] + parts[1]

    def narrow(square):
        return jnp.concatenate([square[:32], square[32:]], axis=1)

    def place(chunk, lines):
        rows = lines.shape[0] // 2
        partial[chunk, 0] = lines[:rows]
        partial[chunk, 1] = lines[rows:]

    def to_twin(chunk):
        copy = pltpu.make_async_remote_copy(
            src_ref=partial.at[chunk, 1 - sub],
            dst_ref=landed.at[chunk],
            send_sem=core_send.at[chunk],
            recv_sem=core_recv.at[chunk],
            device_id=twin,
            device_id_type=MESH,
        )
        copy.start()
        return copy

    def to_snaps(chunk):
        copies = []
        for k in range(1, snaps):
            copy = pltpu.make_async_remote_copy(
                src_ref=snaps_sum.at[chunk, snap],
                dst_ref=snaps_sum.at[chunk, snap],
                send_sem=snap_send.at[chunk, k - 1],
                recv_sem=snap_recv.at[chunk, k - 1],
                device_id=snap_peers[k - 1],
                device_id_type=MESH,
            )
            copy.start()
            copies.append(copy)
        return copies

    def to_both(chunk):
        copy = pltpu.make_async_remote_copy(
            src_ref=total.at[chunk, sub],
            dst_ref=total.at[chunk, sub],
            send_sem=gather_send.at[chunk],
            recv_sem=gather_recv.at[chunk],
            device_id=twin,
            device_id_type=MESH,
        )
        copy.start()
        return copy

    last, first = slice(0, 2 * rest), slice(2 * rest, 2 * features)
    side = folded(first, last)
    square = folded(first, first)
    head = jnp.concatenate([square, side[:, :cut]], axis=1)
    place(0, jnp.concatenate([head, narrow(side[:, cut:])], axis=0))
    twins = [to_twin(0)]
    square = folded(last, last)
    place(1, jnp.concatenate([square[:cut], narrow(square[cut:, cut:])], axis=0))
    twins.append(to_twin(1))
    spread = []
    for chunk in range(2):
        twins[chunk].wait()
        snaps_sum[chunk, snap] = partial[chunk, sub] + landed[chunk]
        spread.append(to_snaps(chunk))
    gathers = []
    for chunk in range(2):
        for copy in spread[chunk]:
            copy.wait()
        block = snaps_sum[chunk, 0]
        for k in range(1, snaps):
            block = block + snaps_sum[chunk, k]
        total[chunk, sub] = block
        gathers.append(to_both(chunk))
    for chunk in range(2):
        gathers[chunk].wait()
        chunks_ref[chunk] = total[chunk].reshape(chunks_ref.shape[1:])


def gram_kernel(
    counts,
    fields_in,
    ids_in,
    weight_in,
    terms_in,
    mix_in,
    packed_ref,
    feature_out,
    fields_ref,
    ids_ref,
    weight_ref,
    terms_ref,
    mix_ref,
    load_done,
    feature_ref,
    gram_wide,
    halo_z,
    halo_x,
    natural,
    partial,
    landed,
    snaps_sum,
    total,
    halo_send,
    halo_recv,
    plane_send,
    plane_recv,
    snap_send,
    snap_recv,
    gather_send,
    gather_recv,
):
    slabs, subs, snaps = counts
    plane = slabs * subs
    slab, sub, snap = lax.axis_index("slab"), lax.axis_index("sub"), lax.axis_index("snap")
    me = slab * subs + sub
    plane_peers = [plane_device(lax.rem(me + k, plane), subs) for k in range(1, plane)]
    snap_peers = [{"snap": lax.rem(snap + k, snaps)} for k in range(1, snaps)]

    loads = [
        pltpu.make_async_copy(source, target, load_done.at[k])
        for k, (source, target) in enumerate(
            (
                (fields_in, fields_ref),
                (terms_in, terms_ref),
                (mix_in, mix_ref),
                (weight_in, weight_ref),
                (ids_in, ids_ref),
            )
        )
    ]
    for load in loads:
        load.start()
    barrier = pltpu.get_barrier_semaphore()
    for peer in plane_peers + snap_peers:
        pl.semaphore_signal(barrier, inc=1, device_id=peer, device_id_type=MESH)
    for load in loads:
        load.wait()
    features = terms_ref.shape[1]
    field_count, layers, columns, width = fields_ref.shape[1:]
    cells_rows = layers * columns
    choose, mix = selection(features, terms_ref, mix_ref)
    table = lax.broadcasted_iota(jnp.int32, weight_ref.shape, 1)
    scale = jnp.sum(
        jnp.where(table == ids_ref[...], weight_ref[...], 0.0), axis=1, keepdims=True
    )
    natural[28 * cells_rows :, :] = jnp.zeros((4 * cells_rows, width), jnp.float32)

    def put(field, kind, layer, tile):
        start = (field * 7 + kind) * cells_rows + layer * columns
        natural[start : start + columns, :] = tile

    for f in range(field_count):
        for z in range(layers):
            tile = fields_ref[0, f, z]
            put(f, 0, z, tile)
            y_shifts = [pltpu.roll(tile, s % width, 1) for s in (-1, 1, -2, 2)]
            first, second = pair(tile, *y_shifts)
            put(f, 3, z, first)
            put(f, 6, z, second)

    pl.semaphore_wait(barrier, len(plane_peers) + len(snap_peers))

    copies = []
    for axis, index, count, halo, base in (
        ("slab", slab, slabs, halo_z, 0),
        ("sub", sub, subs, halo_x, 2),
    ):
        for side, move in ((0, 1), (1, count - 1))[: 1 if count == 2 else 2]:
            copy = pltpu.make_async_remote_copy(
                src_ref=fields_ref.at[0],
                dst_ref=halo.at[side],
                send_sem=halo_send.at[base + side],
                recv_sem=halo_recv.at[base + side],
                device_id={axis: lax.rem(index + move, count)},
                device_id_type=MESH,
            )
            copy.start()
            copies.append(copy)

    for copy in copies:
        copy.wait()

    z_low, z_high = 0, 0 if slabs == 2 else 1
    x_low, x_high = 0, 0 if subs == 2 else 1
    line = lax.broadcasted_iota(jnp.int32, (columns, width), 0)
    for f in range(field_count):
        column = [halo_z[z_low, f, z] for z in range(layers)]
        column += [fields_ref[0, f, z] for z in range(layers)]
        column += [halo_z[z_high, f, z] for z in range(layers)]
        for z in range(layers):
            tile = column[layers + z]
            at = layers + z
            first, second = pair(
                tile, column[at + 1], column[at - 1], column[at + 2], column[at - 2]
            )
            put(f, 1, z, first)
            put(f, 4, z, second)
            low, high = halo_x[x_low, f, z], halo_x[x_high, f, z]
            shifts = []
            for s in (-1, 1, -2, 2):
                turned = pltpu.roll(tile, s % columns, 0)
                other = pltpu.roll(high if s < 0 else low, s % columns, 0)
                inside = line < columns + s if s < 0 else line >= s
                shifts.append(jnp.where(inside, turned, other))
            first, second = pair(tile, *shifts)
            put(f, 2, z, first)
            put(f, 5, z, second)

    for start in range(0, cells_rows, 2):
        lanes = slice(start * width, (start + 2) * width)
        values = picked_products(natural, start, choose, scale, mix)
        feature_ref[:, lanes] = values
        store_features(feature_out, values, lanes)

    everything = feature_ref[...]
    wide = gram_wide.shape[1]
    gram_wide[:, :features] = lax.dot_general(
        everything,
        everything,
        (((1,), (1,)), ((), ())),
        precision=HIGHEST,
        preferred_element_type=jnp.float32,
    )
    half = features // 2
    above = gram_wide[:half, :]
    below = gram_wide[half:, :]
    row = lax.broadcasted_iota(jnp.int32, (half, wide), 0)
    lane = lax.broadcasted_iota(jnp.int32, (half, wide), 1)
    corner = jnp.sum(jnp.where(lane == row + half, below, 0.0), axis=1, keepdims=True)
    packed = jnp.where(
        lane < half,
        jnp.where(lane >= row, above, pltpu.roll(below, wide - half, 1)),
        jnp.where(lane < features, above, corner),
    )
    rows = half // plane
    for k in range(plane):
        partial[k] = packed[k * rows : (k + 1) * rows, :]

    copies = []
    for k in range(1, plane):
        copy = pltpu.make_async_remote_copy(
            src_ref=partial.at[lax.rem(me + k, plane)],
            dst_ref=landed.at[k - 1],
            send_sem=plane_send.at[k - 1],
            recv_sem=plane_recv.at[k - 1],
            device_id=plane_peers[k - 1],
            device_id_type=MESH,
        )
        copy.start()
        copies.append(copy)
    block = partial[me]
    for k in range(1, plane):
        copies[k - 1].wait()
        block = block + landed[k - 1]
    snaps_sum[snap] = block

    copies = []
    for k in range(1, snaps):
        copy = pltpu.make_async_remote_copy(
            src_ref=snaps_sum.at[snap],
            dst_ref=snaps_sum.at[snap],
            send_sem=snap_send.at[k - 1],
            recv_sem=snap_recv.at[k - 1],
            device_id=snap_peers[k - 1],
            device_id_type=MESH,
        )
        copy.start()
        copies.append(copy)
    for copy in copies:
        copy.wait()
    block = snaps_sum[0]
    for k in range(1, snaps):
        block = block + snaps_sum[k]
    total[me] = block

    copies = []
    for k in range(1, plane):
        copy = pltpu.make_async_remote_copy(
            src_ref=total.at[me],
            dst_ref=total.at[me],
            send_sem=gather_send.at[k - 1],
            recv_sem=gather_recv.at[k - 1],
            device_id=plane_peers[k - 1],
            device_id_type=MESH,
        )
        copy.start()
        copies.append(copy)
    for copy in copies:
        copy.wait()
    for k in range(plane):
        packed_ref[k * rows : (k + 1) * rows, :] = total[k]


def local(fields, snap_ids, snap_weight, product_terms, mix_weight):
    counts = tuple(lax.axis_size(axis) for axis in ("slab", "sub", "snap"))
    slabs, subs, snaps = counts
    plane = slabs * subs
    field_count, layers, columns, width = fields.shape[1:]
    features = product_terms.shape[0]
    cells = layers * columns * width
    half = features // 2
    rows = half // plane
    wide = features // 128 * 128 + 128
    f32 = jnp.float32
    in_vmem = pl.BlockSpec(memory_space=pltpu.VMEM)
    in_hbm = pl.BlockSpec(memory_space=pltpu.HBM)
    dma = pltpu.SemaphoreType.DMA
    operands = (
        fields,
        snap_ids.reshape(1, 1),
        snap_weight.reshape(1, -1),
        product_terms.T,
        mix_weight.reshape(1, -1),
    )
    tables = [
        pltpu.VMEM((1, 1), jnp.int32),
        pltpu.VMEM((1, snap_weight.shape[0]), f32),
        pltpu.VMEM((3, features), jnp.int32),
        pltpu.VMEM((1, features), f32),
        dma((5,)),
    ]
    pairs = pltpu.VMEM((2 * features, cells), jnp.bfloat16)
    bases = pltpu.VMEM((32 * layers * columns, width), f32)
    if (slabs, subs, features) == (2, 2, 3 * feature_cut):
        load_gram = load_chunks
        part = pltpu.VMEM((2, 2, 48, 128), f32)
        gram, values = pl.pallas_call(
            functools.partial(twin_kernel, snaps),
            out_shape=(pltpu.VMEM((2, 96, 128), f32), pairs),
            in_specs=[in_hbm] * 5,
            out_specs=(in_vmem, in_vmem),
            scratch_shapes=[pltpu.VMEM((4,) + fields.shape[1:], f32)]
            + tables
            + [
                pairs,
                bases,
                bases,
                part,
                pltpu.VMEM((2, 48, 128), f32),
                pltpu.VMEM((2, snaps, 48, 128), f32),
                part,
                dma((3,)),
                dma((3,)),
                dma((2,)),
                dma((2,)),
                dma((2, snaps - 1)),
                dma((2, snaps - 1)),
                dma((2,)),
                dma((2,)),
            ],
            compiler_params=pltpu.CompilerParams(collective_id=0, has_side_effects=True),
        )(*operands)
    else:
        load_gram = load_packed
        gram, values = pl.pallas_call(
            functools.partial(gram_kernel, counts),
            out_shape=(pltpu.VMEM((half, wide), f32), pairs),
            in_specs=[in_hbm] * 5,
            out_specs=(in_vmem, in_vmem),
            scratch_shapes=[pltpu.VMEM(fields.shape, f32)]
            + tables
            + [
                pltpu.VMEM((features, cells), f32),
                pltpu.VMEM((features, wide), f32),
                pltpu.VMEM((2,) + fields.shape[1:], f32),
                pltpu.VMEM((2,) + fields.shape[1:], f32),
                bases,
                pltpu.VMEM((plane, rows, wide), f32),
                pltpu.VMEM((plane - 1, rows, wide), f32),
                pltpu.VMEM((snaps, rows, wide), f32),
                pltpu.VMEM((plane, rows, wide), f32),
                dma((4,)),
                dma((4,)),
                dma((plane - 1,)),
                dma((plane - 1,)),
                dma((snaps - 1,)),
                dma((snaps - 1,)),
                dma((plane - 1,)),
                dma((plane - 1,)),
            ],
            compiler_params=pltpu.CompilerParams(collective_id=0, has_side_effects=True),
        )(*operands)
    whitened, r_factor = pl.pallas_call(
        functools.partial(whiten_kernel, float(snaps * plane * cells), load_gram),
        out_shape=(
            jax.ShapeDtypeStruct((1, features, layers, columns, width), jnp.bfloat16),
            jax.ShapeDtypeStruct((features, features), f32),
        ),
        in_specs=[in_vmem, in_vmem],
        out_specs=(in_vmem, in_vmem),
        scratch_shapes=[
            pltpu.VMEM((features, 2 * wide), f32),
            pltpu.VMEM((features * (cells // 128), 128), f32),
        ],
        compiler_params=pltpu.CompilerParams(vmem_limit_bytes=24 * 1024 * 1024),
    )(
        pltpu.with_memory_space_constraint(gram, pltpu.VMEM),
        pltpu.with_memory_space_constraint(values, pltpu.VMEM),
    )
    return (whitened, r_factor)


def solution(mesh):
    return jax.shard_map(
        local,
        mesh=mesh,
        in_specs=(
            P(("groups", "snap"), None, "slab", "sub", None),
            P(("groups", "snap")),
            P(),
            P(),
            P(),
        ),
        out_specs=(P(("groups", "snap"), None, "slab", "sub", None), P("groups", None)),
        check_vma=False,
    )
```

```python
import functools

import jax
import jax.numpy as jnp
from jax import lax
from jax.experimental import pallas as pl
from jax.experimental.pallas import tpu as pltpu
from jax.sharding import PartitionSpec as P

ridge_value = 0.05
panel_rows = 64
feature_cut = 64
beside_group = 2
HIGHEST = lax.Precision.HIGHEST
MESH = pl.DeviceIdType.MESH


def split(values, count):
    parts = []
    for _ in range(count):
        part = values.astype(jnp.bfloat16)
        parts.append(part)
        values = values - part.astype(jnp.float32)
    return parts


def row_of(tile, place):
    return jnp.broadcast_to(tile[place : place + 1, :], tile.shape)


def eliminate_group(groups, first, place):
    line = lax.broadcasted_iota(jnp.int32, (8, 128), 0)
    lane_tile, lane = place // 128, place % 128
    later = range(first, len(groups))
    spread = {
        (r, c): jnp.take_along_axis(
            groups[r][lane_tile], jnp.full((8, 128), lane + c, jnp.int32), axis=1
        )
        for r in later
        for c in range(8)
    }
    pivots = jnp.ones((8, 128), jnp.float32)
    factors = []
    for j in range(8):
        pivot = row_of(spread[first, j], j)
        pivots = jnp.where(line == j, pivot, pivots)
        inverse = 1.0 / pivot
        scaled = {r: spread[r, j] * inverse for r in later}
        scaled[first] = jnp.where(line > j, scaled[first], 0.0)
        factors.append(scaled)
        for c in range(j + 1, 8):
            head = row_of(spread[first, c], j)
            for r in later:
                spread[r, c] = spread[r, c] - scaled[r] * head
    for t in range(len(groups[first])):
        tile = groups[first][t]
        for j in range(8):
            head = row_of(tile, j)
            if j < 7:
                tile = tile - factors[j][first] * head
            for r in later:
                if r > first:
                    groups[r][t] = groups[r][t] - factors[j][r] * head
        groups[first][t] = tile
    return 1.0 / jnp.sqrt(pivots)


def panel_lanes(work, start):
    half = work.shape[1] // 2
    return start // 128 * 128, half + (start + panel_rows + 127) // 128 * 128


def eliminate_panel(work, start, beside):
    low, high = panel_lanes(work, start)
    stop = start + panel_rows
    groups = [
        [work[r : r + 8, t : t + 128] for t in range(low, high, 128)] for r in range(start, stop, 8)
    ]
    for g in range(panel_rows // 8):
        scale = eliminate_group(groups, g, start + 8 * g - low)
        row = start + 8 * g
        work[row : row + 8, low:high] = jnp.concatenate([tile * scale for tile in groups[g]], axis=1)
        beside(g)


def update_below(work, start, order):
    low, high = panel_lanes(work, start)
    half = work.shape[1] // 2
    stop = start + panel_rows
    panel = work[start:stop, low:high]
    sides = panel[:, : half - low].T[stop - low : order - low, :]
    a, b, c = split(sides, 3)
    d, e, f = split(panel, 3)
    left = jnp.concatenate([a, a, b, b, a, c], axis=1)
    right = jnp.concatenate([d, e, d, e, f, d], axis=0)
    work[stop:order, low:high] = work[stop:order, low:high] - jnp.dot(
        left, right, preferred_element_type=jnp.float32
    )


def regularise(work, first, last, cells_total):
    half = work.shape[1] // 2
    rows = lax.broadcasted_iota(jnp.int32, (last - first, half), 0) + first
    columns = lax.broadcasted_iota(jnp.int32, (last - first, half), 1)
    identity = (rows == columns).astype(jnp.float32)
    work[first:last, half:] = identity
    work[first:last, :half] = work[first:last, :half] * (1.0 / cells_total) + ridge_value * identity


def load_packed(packed_ref, work, order):
    middle = packed_ref.shape[0]
    half = work.shape[1] // 2
    row = lax.broadcasted_iota(jnp.int32, (middle, 128), 0)
    lane = lax.broadcasted_iota(jnp.int32, (middle, 128), 1)
    left = packed_ref[:, :128]
    turned = jnp.concatenate([left, jnp.zeros((128 - middle, 128), jnp.float32)], axis=0).T
    turned = turned[:middle, :]
    work[:middle, :128] = jnp.where((lane >= row) | (lane >= middle), left, turned)
    work[:middle, 128:half] = jnp.where(lane + 128 < order, packed_ref[:, 128:], 0.0)
    corner = packed_ref[:, order : order + 1]
    lower = jnp.where(lane < row, left, jnp.where(lane > row, turned, corner))
    lower = jnp.where(lane < middle, lower, 0.0)
    lower = jnp.concatenate([lower, jnp.zeros((middle, half - 128), jnp.float32)], axis=1)
    work[middle:, :half] = pltpu.roll(lower, middle, 1)


def spare(tile):
    lane = lax.broadcasted_iota(jnp.int32, (32, 128), 1)
    near = jnp.where(lane < 64, tile, 0.0)
    far = pltpu.roll(jnp.where(lane >= 64, tile, 0.0), 64, 1)
    return jnp.concatenate([near, far], axis=0)


def load_head(head, work):
    work[:64, :128] = head[:64]
    work[:64, 128:256] = spare(head[64:])


def load_tail(tail, work):
    middle = jnp.concatenate([tail[:64], jnp.zeros((64, 128), jnp.float32)], axis=1)
    work[64:128, :256] = pltpu.roll(middle, 64, 1)
    work[128:192, :128] = jnp.zeros((64, 128), jnp.float32)
    work[128:192, 128:256] = spare(tail[64:])


def whiten_kernel(cells_total, begun, *refs):
    if begun:
        top_ref, tail_ref, feature_ref, *refs = refs
    else:
        packed_ref, feature_ref, *refs = refs
    white_ref, factor_ref, work, spread, white, factor, done = refs
    order = factor.shape[0]
    half = work.shape[1] // 2
    cells = feature_ref.shape[1]
    tiles = cells // 128
    cut, rest = feature_cut, order - feature_cut
    copies = []

    def store(p):
        rows = slice(panel_rows * p, panel_rows * (p + 1))
        for k, (source, target) in enumerate(
            ((factor.at[rows], factor_ref.at[rows]), (white.at[:, rows], white_ref.at[:, rows]))
        ):
            copy = pltpu.make_async_copy(source, target, done.at[2 * p + k])
            copy.start()
            copies.append(copy)

    def whiten(p):
        first, last = panel_rows * p, panel_rows * (p + 1)
        rows = lax.broadcasted_iota(jnp.int32, (panel_rows, order), 0) + first
        columns = lax.broadcasted_iota(jnp.int32, (panel_rows, order), 1)
        factor[first:last, :] = jnp.where(columns >= rows, work[first:last, :order], 0.0)
        inverse = jnp.where(columns <= rows, work[first:last, half : half + order], 0.0)
        upper, lower = split(inverse, 2)
        far = last - cut
        lines = [slice(2 * rest, 2 * rest + cut), slice(2 * rest + cut, 2 * order)]
        tops = [upper[:, :cut], upper[:, :cut]]
        bottoms = [lower[:, :cut], jnp.zeros((panel_rows, cut), jnp.bfloat16)]
        if far > 0:
            lines = [slice(0, far), slice(rest, rest + far)] + lines
            tops = [upper[:, cut:last], upper[:, cut:last]] + tops
            bottoms = [lower[:, cut:last], jnp.zeros((panel_rows, far), jnp.bfloat16)] + bottoms
        left = jnp.concatenate(
            [jnp.concatenate(tops, axis=1), jnp.concatenate(bottoms, axis=1)], axis=0
        )

        def step(g):
            lanes = slice(256 * g, 256 * g + 256)
            right = jnp.concatenate([feature_ref[part, lanes] for part in lines], axis=0)
            both = jnp.dot(left, right, preferred_element_type=jnp.float32)
            solved = both[:panel_rows] + both[panel_rows:]
            for k in range(2):
                place = first * tiles + 2 * g + k
                spread[pl.ds(place, panel_rows, stride=tiles), :] = solved[:, 128 * k : 128 * k + 128]
            if g == tiles // 2 - 1:
                values = spread[first * tiles : last * tiles, :]
                shape = (1, panel_rows) + white.shape[2:]
                white[:, first:last] = values.reshape(shape).astype(white.dtype)
                store(p)

        return step

    def nothing(g):
        pass

    if begun:
        work[:panel_rows, :] = top_ref[...]
        load_tail(tail_ref, work)
        regularise(work, panel_rows, order, cells_total)
    else:
        load_packed(packed_ref, work, order)
        regularise(work, 0, order, cells_total)
        eliminate_panel(work, 0, nothing)
    panels = order // panel_rows
    for p in range(1, panels):
        update_below(work, panel_rows * (p - 1), order)
        eliminate_panel(work, panel_rows * p, whiten(p - 1))
    step = whiten(panels - 1)
    for g in range(tiles // 2):
        step(g)
    for copy in copies:
        copy.wait()


def plane_device(place, subs):
    return {"slab": lax.div(place, subs), "sub": lax.rem(place, subs)}


def store_features(feature_ref, values, lanes):
    cut, rest = feature_cut, values.shape[0] - feature_cut
    upper, lower = split(values, 2)
    feature_ref[:rest, lanes] = upper[cut:]
    feature_ref[rest : 2 * rest, lanes] = lower[cut:]
    feature_ref[2 * rest : 2 * rest + cut, lanes] = upper[:cut]
    feature_ref[2 * rest + cut :, lanes] = lower[:cut]


def pair(center, ahead_one, behind_one, ahead_two, behind_two):
    first = 8.0 * (ahead_one - behind_one) - (ahead_two - behind_two)
    second = 16.0 * (ahead_one + behind_one) - (ahead_two + behind_two) - 30.0 * center
    return first * (1.0 / 12.0), second * (1.0 / 12.0)


def selection(features, terms_ref, mix_ref):
    square_rows = lax.broadcasted_iota(jnp.int32, (features, features), 0)
    square_columns = lax.broadcasted_iota(jnp.int32, (features, features), 1)

    def upright(row):
        return jnp.sum(jnp.where(square_rows == square_columns, row, 0.0), axis=1, keepdims=True)

    slot = lax.broadcasted_iota(jnp.int32, (features, 256), 1)
    base_of = lax.rem(slot, 32).astype(jnp.float32)
    left, middle, right = [
        (upright(terms_ref[k : k + 1, :].astype(jnp.float32)) == base_of).astype(jnp.float32)
        for k in range(3)
    ]
    first, second, third = [part.astype(jnp.float32) for part in split(upright(mix_ref[...]), 3)]
    weights = jnp.where(slot < 96, first, jnp.where(slot < 192, second, third))
    left = jnp.where(slot < 96, left, 0.0)
    middle = jnp.where(slot < 96, middle, 0.0)
    right = jnp.where(slot < 224, right * weights, 0.0)
    return jnp.concatenate([left, middle + right], axis=0).astype(jnp.bfloat16)


def picked_products(natural, start, choose, scale):
    features = choose.shape[0] // 2
    cells_rows = natural.shape[0] // 32
    pieces = []
    for at in (start, start + 1):
        parts = split(natural[pl.ds(at, 32, stride=cells_rows), :], 3)
        pieces.append(jnp.concatenate(parts + parts + [parts[0], parts[0]], axis=0))
    picked = jnp.dot(
        choose, jnp.concatenate(pieces, axis=1), preferred_element_type=jnp.float32
    )
    return scale * picked[:features] * picked[features:]


def products(left, right):
    return lax.dot_general(
        left, right, (((1,), (1,)), ((), ())), preferred_element_type=jnp.float32
    )


def twin_kernel(
    snaps,
    cells_total,
    fields_in,
    ids_in,
    weight_in,
    terms_in,
    mix_in,
    top_ref,
    tail_ref,
    feature_ref,
    blocks,
    ids_ref,
    weight_ref,
    terms_ref,
    mix_ref,
    load_done,
    other_feature,
    natural,
    other_natural,
    partial,
    landed,
    snaps_sum,
    total,
    halo_send,
    halo_recv,
    core_send,
    core_recv,
    snap_send,
    snap_recv,
    gather_send,
    gather_recv,
):
    slab, sub, snap = lax.axis_index("slab"), lax.axis_index("sub"), lax.axis_index("snap")
    twin = {"sub": 1 - sub}
    across = {"slab": 1 - slab}
    corner = {"slab": 1 - slab, "sub": 1 - sub}
    snap_peers = [{"snap": lax.rem(snap + k, snaps)} for k in range(1, snaps)]
    passed = [lax.convert_element_type(snap <= k, jnp.int32) for k in range(snaps - 1)]
    barrier = pltpu.get_barrier_semaphore()
    for peer in [across, corner, twin] + snap_peers:
        pl.semaphore_signal(barrier, inc=1, device_id=peer, device_id_type=MESH)
    loads = [
        pltpu.make_async_copy(source, target, load_done.at[k])
        for k, (source, target) in enumerate(
            (
                (fields_in, blocks.at[pl.ds(0, 1)]),
                (terms_in, terms_ref),
                (mix_in, mix_ref),
                (weight_in, weight_ref),
                (ids_in, ids_ref),
            )
        )
    ]
    for load in loads:
        load.start()
    loads[0].wait()
    pl.semaphore_wait(barrier, 3 + len(snap_peers))
    halos = []
    for slot, peer in ((1, across), (3, corner), (2, twin)):
        copy = pltpu.make_async_remote_copy(
            src_ref=blocks.at[0],
            dst_ref=blocks.at[slot],
            send_sem=halo_send.at[slot - 1],
            recv_sem=halo_recv.at[slot - 1],
            device_id=peer,
            device_id_type=MESH,
        )
        copy.start()
        halos.append(copy)
    for load in loads[1:]:
        load.wait()
    features = terms_ref.shape[1]
    field_count, layers, columns, width = blocks.shape[1:]
    cells_rows = layers * columns
    choose = selection(features, terms_ref, mix_ref)
    table = lax.broadcasted_iota(jnp.int32, weight_ref.shape, 1)
    scale = jnp.sum(
        jnp.where(table == ids_ref[...], weight_ref[...], 0.0), axis=1, keepdims=True
    )
    line = lax.broadcasted_iota(jnp.int32, (columns, width), 0)

    def put(target, field, kind, layer, tile):
        start = (field * 7 + kind) * cells_rows + layer * columns
        target[start : start + columns, :] = tile

    def along_y(target, block):
        target[28 * cells_rows :, :] = jnp.zeros((4 * cells_rows, width), jnp.float32)
        for f in range(field_count):
            for z in range(layers):
                tile = blocks[block, f, z]
                put(target, f, 0, z, tile)
                first, second = pair(tile, *[pltpu.roll(tile, s % width, 1) for s in (-1, 1, -2, 2)])
                put(target, f, 3, z, first)
                put(target, f, 6, z, second)

    def along_x(target, block, beside):
        for f in range(field_count):
            for z in range(layers):
                tile, other = blocks[block, f, z], blocks[beside, f, z]
                shifts = []
                for s in (-1, 1, -2, 2):
                    inside = line < columns + s if s < 0 else line >= s
                    shifts.append(
                        jnp.where(
                            inside,
                            pltpu.roll(tile, s % columns, 0),
                            pltpu.roll(other, s % columns, 0),
                        )
                    )
                first, second = pair(tile, *shifts)
                put(target, f, 2, z, first)
                put(target, f, 5, z, second)

    def along_z(target, block, beside):
        for f in range(field_count):
            column = [blocks[beside, f, z] for z in range(layers)]
            column = column + [blocks[block, f, z] for z in range(layers)] + column
            for z in range(layers):
                at = layers + z
                first, second = pair(
                    column[at], column[at + 1], column[at - 1], column[at + 2], column[at - 2]
                )
                put(target, f, 1, z, first)
                put(target, f, 4, z, second)

    along_y(natural, 0)
    halos[2].wait()
    along_x(natural, 0, 2)
    halos[0].wait()
    along_z(natural, 0, 1)
    for start in range(0, cells_rows, 2):
        values = picked_products(natural, start, choose, scale)
        store_features(feature_ref, values, slice(start * width, (start + 2) * width))
    along_y(other_natural, 1)
    along_z(other_natural, 1, 0)
    halos[1].wait()
    along_x(other_natural, 1, 3)
    for start in range(0, cells_rows, 2):
        values = picked_products(other_natural, start, choose, scale)
        store_features(other_feature, values, slice(start * width, (start + 2) * width))

    cut, rest = feature_cut, features - feature_cut

    def folded(left, right):
        parts = []
        for values in (feature_ref, other_feature):
            both = products(values[left, :], values[right, :])
            high, low = both.shape[0] // 2, both.shape[1] // 2
            both = both[:high] + both[high:]
            parts.append(both[:, :low] + both[:, low:])
        return parts[0] + parts[1]

    def narrow(square):
        return jnp.concatenate([square[:32], square[32:]], axis=1)

    def place(chunk, lines):
        rows = lines.shape[0] // 2
        partial[chunk, 0] = lines[:rows]
        partial[chunk, 1] = lines[rows:]

    def to_twin(chunk):
        copy = pltpu.make_async_remote_copy(
            src_ref=partial.at[chunk, 1 - sub],
            dst_ref=landed.at[chunk],
            send_sem=core_send.at[chunk],
            recv_sem=core_recv.at[chunk],
            device_id=twin,
            device_id_type=MESH,
        )
        copy.start()
        return copy

    def to_snaps(chunk):
        copies = []
        for k in range(snaps - 1):
            copy = pltpu.make_async_remote_copy(
                src_ref=snaps_sum.at[chunk, snap],
                dst_ref=snaps_sum.at[chunk, snap],
                send_sem=snap_send.at[chunk, k],
                recv_sem=snap_recv.at[chunk, lax.rem(snap + snaps - 1 - (k + passed[k]), snaps)],
                device_id={"snap": k + passed[k]},
                device_id_type=MESH,
            )
            copy.start()
            copies.append(copy)
        return copies

    def to_both(chunk):
        copy = pltpu.make_async_remote_copy(
            src_ref=total.at[chunk, sub],
            dst_ref=total.at[chunk, sub],
            send_sem=gather_send.at[chunk],
            recv_sem=gather_recv.at[chunk],
            device_id=twin,
            device_id_type=MESH,
        )
        copy.start()
        return copy

    last, first = slice(0, 2 * rest), slice(2 * rest, 2 * features)
    side = folded(first, last)
    square = folded(first, first)
    head = jnp.concatenate([square, side[:, :cut]], axis=1)
    place(0, jnp.concatenate([head, narrow(side[:, cut:])], axis=0))
    twins = [to_twin(0)]
    square = folded(last, last)
    place(1, jnp.concatenate([square[:cut], narrow(square[cut:, cut:])], axis=0))
    twins.append(to_twin(1))
    spread = []
    for chunk in range(2):
        twins[chunk].wait()
        snaps_sum[chunk, snap] = partial[chunk, sub] + landed[chunk]
        spread.append(to_snaps(chunk))
    gathers = []

    def gather(chunk):
        for copy in spread[chunk]:
            copy.wait()
        block = snaps_sum[chunk, 0]
        for k in range(1, snaps):
            block = block + snaps_sum[chunk, k]
        total[chunk, sub] = block
        gathers.append(to_both(chunk))

    def beside(g):
        if g == beside_group:
            gather(1)

    gather(0)
    gathers[0].wait()
    load_head(total[0].reshape(96, 128), top_ref)
    regularise(top_ref, 0, panel_rows, cells_total)
    eliminate_panel(top_ref, 0, beside)
    gathers[1].wait()
    tail_ref[...] = total[1].reshape(96, 128)


def gram_kernel(
    counts,
    fields_in,
    ids_in,
    weight_in,
    terms_in,
    mix_in,
    packed_ref,
    feature_out,
    fields_ref,
    ids_ref,
    weight_ref,
    terms_ref,
    mix_ref,
    load_done,
    feature_ref,
    gram_wide,
    halo_z,
    halo_x,
    natural,
    partial,
    landed,
    snaps_sum,
    total,
    halo_send,
    halo_recv,
    plane_send,
    plane_recv,
    snap_send,
    snap_recv,
    gather_send,
    gather_recv,
):
    slabs, subs, snaps = counts
    plane = slabs * subs
    slab, sub, snap = lax.axis_index("slab"), lax.axis_index("sub"), lax.axis_index("snap")
    me = slab * subs + sub
    plane_peers = [plane_device(lax.rem(me + k, plane), subs) for k in range(1, plane)]
    snap_peers = [{"snap": lax.rem(snap + k, snaps)} for k in range(1, snaps)]

    loads = [
        pltpu.make_async_copy(source, target, load_done.at[k])
        for k, (source, target) in enumerate(
            (
                (fields_in, fields_ref),
                (terms_in, terms_ref),
                (mix_in, mix_ref),
                (weight_in, weight_ref),
                (ids_in, ids_ref),
            )
        )
    ]
    for load in loads:
        load.start()
    barrier = pltpu.get_barrier_semaphore()
    for peer in plane_peers + snap_peers:
        pl.semaphore_signal(barrier, inc=1, device_id=peer, device_id_type=MESH)
    for load in loads:
        load.wait()
    features = terms_ref.shape[1]
    field_count, layers, columns, width = fields_ref.shape[1:]
    cells_rows = layers * columns
    choose = selection(features, terms_ref, mix_ref)
    table = lax.broadcasted_iota(jnp.int32, weight_ref.shape, 1)
    scale = jnp.sum(
        jnp.where(table == ids_ref[...], weight_ref[...], 0.0), axis=1, keepdims=True
    )
    natural[28 * cells_rows :, :] = jnp.zeros((4 * cells_rows, width), jnp.float32)

    def put(field, kind, layer, tile):
        start = (field * 7 + kind) * cells_rows + layer * columns
        natural[start : start + columns, :] = tile

    for f in range(field_count):
        for z in range(layers):
            tile = fields_ref[0, f, z]
            put(f, 0, z, tile)
            y_shifts = [pltpu.roll(tile, s % width, 1) for s in (-1, 1, -2, 2)]
            first, second = pair(tile, *y_shifts)
            put(f, 3, z, first)
            put(f, 6, z, second)

    pl.semaphore_wait(barrier, len(plane_peers) + len(snap_peers))

    copies = []
    for axis, index, count, halo, base in (
        ("slab", slab, slabs, halo_z, 0),
        ("sub", sub, subs, halo_x, 2),
    ):
        for side, move in ((0, 1), (1, count - 1))[: 1 if count == 2 else 2]:
            copy = pltpu.make_async_remote_copy(
                src_ref=fields_ref.at[0],
                dst_ref=halo.at[side],
                send_sem=halo_send.at[base + side],
                recv_sem=halo_recv.at[base + side],
                device_id={axis: lax.rem(index + move, count)},
                device_id_type=MESH,
            )
            copy.start()
            copies.append(copy)

    for copy in copies:
        copy.wait()

    z_low, z_high = 0, 0 if slabs == 2 else 1
    x_low, x_high = 0, 0 if subs == 2 else 1
    line = lax.broadcasted_iota(jnp.int32, (columns, width), 0)
    for f in range(field_count):
        column = [halo_z[z_low, f, z] for z in range(layers)]
        column += [fields_ref[0, f, z] for z in range(layers)]
        column += [halo_z[z_high, f, z] for z in range(layers)]
        for z in range(layers):
            tile = column[layers + z]
            at = layers + z
            first, second = pair(
                tile, column[at + 1], column[at - 1], column[at + 2], column[at - 2]
            )
            put(f, 1, z, first)
            put(f, 4, z, second)
            low, high = halo_x[x_low, f, z], halo_x[x_high, f, z]
            shifts = []
            for s in (-1, 1, -2, 2):
                turned = pltpu.roll(tile, s % columns, 0)
                other = pltpu.roll(high if s < 0 else low, s % columns, 0)
                inside = line < columns + s if s < 0 else line >= s
                shifts.append(jnp.where(inside, turned, other))
            first, second = pair(tile, *shifts)
            put(f, 2, z, first)
            put(f, 5, z, second)

    for start in range(0, cells_rows, 2):
        lanes = slice(start * width, (start + 2) * width)
        values = picked_products(natural, start, choose, scale)
        feature_ref[:, lanes] = values
        store_features(feature_out, values, lanes)

    everything = feature_ref[...]
    wide = gram_wide.shape[1]
    gram_wide[:, :features] = lax.dot_general(
        everything,
        everything,
        (((1,), (1,)), ((), ())),
        precision=HIGHEST,
        preferred_element_type=jnp.float32,
    )
    half = features // 2
    above = gram_wide[:half, :]
    below = gram_wide[half:, :]
    row = lax.broadcasted_iota(jnp.int32, (half, wide), 0)
    lane = lax.broadcasted_iota(jnp.int32, (half, wide), 1)
    corner = jnp.sum(jnp.where(lane == row + half, below, 0.0), axis=1, keepdims=True)
    packed = jnp.where(
        lane < half,
        jnp.where(lane >= row, above, pltpu.roll(below, wide - half, 1)),
        jnp.where(lane < features, above, corner),
    )
    rows = half // plane
    for k in range(plane):
        partial[k] = packed[k * rows : (k + 1) * rows, :]

    copies = []
    for k in range(1, plane):
        copy = pltpu.make_async_remote_copy(
            src_ref=partial.at[lax.rem(me + k, plane)],
            dst_ref=landed.at[k - 1],
            send_sem=plane_send.at[k - 1],
            recv_sem=plane_recv.at[k - 1],
            device_id=plane_peers[k - 1],
            device_id_type=MESH,
        )
        copy.start()
        copies.append(copy)
    block = partial[me]
    for k in range(1, plane):
        copies[k - 1].wait()
        block = block + landed[k - 1]
    snaps_sum[snap] = block

    copies = []
    for k in range(1, snaps):
        copy = pltpu.make_async_remote_copy(
            src_ref=snaps_sum.at[snap],
            dst_ref=snaps_sum.at[snap],
            send_sem=snap_send.at[k - 1],
            recv_sem=snap_recv.at[k - 1],
            device_id=snap_peers[k - 1],
            device_id_type=MESH,
        )
        copy.start()
        copies.append(copy)
    for copy in copies:
        copy.wait()
    block = snaps_sum[0]
    for k in range(1, snaps):
        block = block + snaps_sum[k]
    total[me] = block

    copies = []
    for k in range(1, plane):
        copy = pltpu.make_async_remote_copy(
            src_ref=total.at[me],
            dst_ref=total.at[me],
            send_sem=gather_send.at[k - 1],
            recv_sem=gather_recv.at[k - 1],
            device_id=plane_peers[k - 1],
            device_id_type=MESH,
        )
        copy.start()
        copies.append(copy)
    for copy in copies:
        copy.wait()
    for k in range(plane):
        packed_ref[k * rows : (k + 1) * rows, :] = total[k]


def local(fields, snap_ids, snap_weight, product_terms, mix_weight):
    counts = tuple(lax.axis_size(axis) for axis in ("slab", "sub", "snap"))
    slabs, subs, snaps = counts
    plane = slabs * subs
    field_count, layers, columns, width = fields.shape[1:]
    features = product_terms.shape[0]
    cells = layers * columns * width
    cells_total = float(snaps * plane * cells)
    half = features // 2
    rows = half // plane
    wide = features // 128 * 128 + 128
    f32 = jnp.float32
    in_vmem = pl.BlockSpec(memory_space=pltpu.VMEM)
    in_hbm = pl.BlockSpec(memory_space=pltpu.HBM)
    dma = pltpu.SemaphoreType.DMA
    operands = (
        fields,
        snap_ids.reshape(1, 1),
        snap_weight.reshape(1, -1),
        product_terms.T,
        mix_weight.reshape(1, -1),
    )
    tables = [
        pltpu.VMEM((1, 1), jnp.int32),
        pltpu.VMEM((1, snap_weight.shape[0]), f32),
        pltpu.VMEM((3, features), jnp.int32),
        pltpu.VMEM((1, features), f32),
        dma((5,)),
    ]
    pairs = pltpu.VMEM((2 * features, cells), jnp.bfloat16)
    bases = pltpu.VMEM((32 * layers * columns, width), f32)
    if (slabs, subs, features) == (2, 2, 3 * feature_cut):
        part = pltpu.VMEM((2, 2, 48, 128), f32)
        results = pl.pallas_call(
            functools.partial(twin_kernel, snaps, cells_total),
            out_shape=(pltpu.VMEM((panel_rows, 2 * wide), f32), pltpu.VMEM((96, 128), f32), pairs),
            in_specs=[in_hbm] * 5,
            out_specs=(in_vmem,) * 3,
            scratch_shapes=[pltpu.VMEM((4,) + fields.shape[1:], f32)]
            + tables
            + [
                pairs,
                bases,
                bases,
                part,
                pltpu.VMEM((2, 48, 128), f32),
                pltpu.VMEM((2, snaps, 48, 128), f32),
                part,
                dma((3,)),
                dma((3,)),
                dma((2,)),
                dma((2,)),
                dma((2, snaps - 1)),
                dma((2, snaps - 1)),
                dma((2,)),
                dma((2,)),
            ],
            compiler_params=pltpu.CompilerParams(collective_id=0, has_side_effects=True),
        )(*operands)
    else:
        results = pl.pallas_call(
            functools.partial(gram_kernel, counts),
            out_shape=(pltpu.VMEM((half, wide), f32), pairs),
            in_specs=[in_hbm] * 5,
            out_specs=(in_vmem, in_vmem),
            scratch_shapes=[pltpu.VMEM(fields.shape, f32)]
            + tables
            + [
                pltpu.VMEM((features, cells), f32),
                pltpu.VMEM((features, wide), f32),
                pltpu.VMEM((2,) + fields.shape[1:], f32),
                pltpu.VMEM((2,) + fields.shape[1:], f32),
                bases,
                pltpu.VMEM((plane, rows, wide), f32),
                pltpu.VMEM((plane - 1, rows, wide), f32),
                pltpu.VMEM((snaps, rows, wide), f32),
                pltpu.VMEM((plane, rows, wide), f32),
                dma((4,)),
                dma((4,)),
                dma((plane - 1,)),
                dma((plane - 1,)),
                dma((snaps - 1,)),
                dma((snaps - 1,)),
                dma((plane - 1,)),
                dma((plane - 1,)),
            ],
            compiler_params=pltpu.CompilerParams(collective_id=0, has_side_effects=True),
        )(*operands)
    white = (1, features, layers, columns, width)
    return pl.pallas_call(
        functools.partial(whiten_kernel, cells_total, len(results) == 3),
        out_shape=(
            jax.ShapeDtypeStruct(white, jnp.bfloat16),
            jax.ShapeDtypeStruct((features, features), f32),
        ),
        in_specs=[in_vmem] * len(results),
        out_specs=(in_hbm, in_hbm),
        scratch_shapes=[
            pltpu.VMEM((features, 2 * wide), f32),
            pltpu.VMEM((features * (cells // 128), 128), f32),
            pltpu.VMEM(white, jnp.bfloat16),
            pltpu.VMEM((features, features), f32),
            dma((2 * features // panel_rows,)),
        ],
        compiler_params=pltpu.CompilerParams(vmem_limit_bytes=24 * 1024 * 1024),
    )(*[pltpu.with_memory_space_constraint(value, pltpu.VMEM) for value in results])


def solution(mesh):
    return jax.shard_map(
        local,
        mesh=mesh,
        in_specs=(
            P(("groups", "snap"), None, "slab", "sub", None),
            P(("groups", "snap")),
            P(),
            P(),
            P(),
        ),
        out_specs=(P(("groups", "snap"), None, "slab", "sub", None), P("groups", None)),
        check_vma=False,
    )
```

```python
import functools

import jax
import jax.numpy as jnp
from jax import lax
from jax.experimental import pallas as pl
from jax.experimental.pallas import tpu as pltpu
from jax.sharding import PartitionSpec as P

ridge_value = 0.05
panel_rows = 64
feature_cut = 64
beside_group = 1
HIGHEST = lax.Precision.HIGHEST
MESH = pl.DeviceIdType.MESH


def split(values, count):
    parts = []
    for _ in range(count):
        part = values.astype(jnp.bfloat16)
        parts.append(part)
        values = values - part.astype(jnp.float32)
    return parts


def row_of(tile, place):
    return jnp.broadcast_to(tile[place : place + 1, :], tile.shape)


def eliminate_group(groups, first, place):
    line = lax.broadcasted_iota(jnp.int32, (8, 128), 0)
    lane_tile, lane = place // 128, place % 128
    later = range(first, len(groups))
    spread = {
        (r, c): jnp.take_along_axis(
            groups[r][lane_tile], jnp.full((8, 128), lane + c, jnp.int32), axis=1
        ) if r == first else jnp.broadcast_to(groups[r][lane_tile][:, lane + c : lane + c + 1], (8, 128))
        for r in later
        for c in range(8)
    }
    pivots = jnp.ones((8, 128), jnp.float32)
    factors = []
    head = {(j, c): row_of(spread[first, c], j) for c in range(8) for j in range(c + 1)}
    inverses = []
    for j in range(0, 8, 2):
        k = j + 1
        one, cross, two = head[j, j], head[j, k], head[k, k]
        first_inverse = 1.0 / one
        product = one * two - cross * cross
        second_inverse = one * (1.0 / product)
        pivots = jnp.where(line == j, one, pivots)
        pivots = jnp.where(line == k, product * first_inverse, pivots)
        ratio = cross * first_inverse
        for c in range(j + 2, 8):
            head[k, c] = head[k, c] - head[j, c] * ratio
        for c in range(j + 2, 8):
            left, right = head[j, c] * first_inverse, head[k, c] * second_inverse
            for d in range(c, 8):
                head[c, d] = (head[c, d] - left * head[j, d]) - right * head[k, d]
        inverses += [first_inverse, second_inverse]
    for j in range(8):
        inverse = inverses[j]
        scaled = {r: spread[r, j] * inverse for r in later}
        scaled[first] = jnp.where(line > j, scaled[first], 0.0)
        factors.append(scaled)
        for c in range(j + 1, 8):
            for r in later:
                spread[r, c] = spread[r, c] - scaled[r] * head[j, c]
    for t in range(len(groups[first])):
        tile = groups[first][t]
        for j in range(8):
            row = row_of(tile, j)
            if j < 7:
                tile = tile - factors[j][first] * row
            for r in later:
                if r > first:
                    groups[r][t] = groups[r][t] - factors[j][r] * row
        groups[first][t] = tile
    return 1.0 / jnp.sqrt(pivots)


def panel_lanes(work, start):
    half = work.shape[1] // 2
    return start // 128 * 128, half + (start + panel_rows + 127) // 128 * 128


def eliminate_panel(work, start, beside):
    low, high = panel_lanes(work, start)
    stop = start + panel_rows
    groups = [
        [work[r : r + 8, t : t + 128] for t in range(low, high, 128)] for r in range(start, stop, 8)
    ]
    for g in range(panel_rows // 8):
        scale = eliminate_group(groups, g, start + 8 * g - low)
        row = start + 8 * g
        work[row : row + 8, low:high] = jnp.concatenate([tile * scale for tile in groups[g]], axis=1)
        beside(g)


def update_below(work, start, order):
    low, high = panel_lanes(work, start)
    half = work.shape[1] // 2
    stop = start + panel_rows
    panel = work[start:stop, low:high]
    sides = panel[:, : half - low].T[stop - low : order - low, :]
    a, b, c = split(sides, 3)
    d, e, f = split(panel, 3)
    left = jnp.concatenate([a, a, b, b, a, c], axis=1)
    right = jnp.concatenate([d, e, d, e, f, d], axis=0)
    work[stop:order, low:high] = work[stop:order, low:high] - jnp.dot(
        left, right, preferred_element_type=jnp.float32
    )


def regularise(work, first, last, cells_total):
    half = work.shape[1] // 2
    rows = lax.broadcasted_iota(jnp.int32, (last - first, half), 0) + first
    columns = lax.broadcasted_iota(jnp.int32, (last - first, half), 1)
    identity = (rows == columns).astype(jnp.float32)
    work[first:last, half:] = identity
    work[first:last, :half] = work[first:last, :half] * (1.0 / cells_total) + ridge_value * identity


def load_packed(packed_ref, work, order):
    middle = packed_ref.shape[0]
    half = work.shape[1] // 2
    row = lax.broadcasted_iota(jnp.int32, (middle, 128), 0)
    lane = lax.broadcasted_iota(jnp.int32, (middle, 128), 1)
    left = packed_ref[:, :128]
    turned = jnp.concatenate([left, jnp.zeros((128 - middle, 128), jnp.float32)], axis=0).T
    turned = turned[:middle, :]
    work[:middle, :128] = jnp.where((lane >= row) | (lane >= middle), left, turned)
    work[:middle, 128:half] = jnp.where(lane + 128 < order, packed_ref[:, 128:], 0.0)
    corner = packed_ref[:, order : order + 1]
    lower = jnp.where(lane < row, left, jnp.where(lane > row, turned, corner))
    lower = jnp.where(lane < middle, lower, 0.0)
    lower = jnp.concatenate([lower, jnp.zeros((middle, half - 128), jnp.float32)], axis=1)
    work[middle:, :half] = pltpu.roll(lower, middle, 1)


def spare(tile):
    lane = lax.broadcasted_iota(jnp.int32, (32, 128), 1)
    near = jnp.where(lane < 64, tile, 0.0)
    far = pltpu.roll(jnp.where(lane >= 64, tile, 0.0), 64, 1)
    return jnp.concatenate([near, far], axis=0)


def load_head(head, work):
    work[:64, :128] = head[:64]
    work[:64, 128:256] = spare(head[64:])


def load_tail(tail, work):
    middle = jnp.concatenate([tail[:64], jnp.zeros((64, 128), jnp.float32)], axis=1)
    work[64:128, :256] = pltpu.roll(middle, 64, 1)
    work[128:192, :128] = jnp.zeros((64, 128), jnp.float32)
    work[128:192, 128:256] = spare(tail[64:])


def whiten_kernel(cells_total, begun, *refs):
    if begun:
        top_ref, tail_ref, feature_ref, *refs = refs
    else:
        packed_ref, feature_ref, *refs = refs
    white_ref, factor_ref, work, spread, white, factor, done = refs
    order = factor.shape[0]
    half = work.shape[1] // 2
    cells = feature_ref.shape[1]
    tiles = cells // 128
    cut, rest = feature_cut, order - feature_cut
    copies = []

    def store(p):
        rows = slice(panel_rows * p, panel_rows * (p + 1))
        for k, (source, target) in enumerate(
            ((factor.at[rows], factor_ref.at[rows]), (white.at[:, rows], white_ref.at[:, rows]))
        ):
            copy = pltpu.make_async_copy(source, target, done.at[2 * p + k])
            copy.start()
            copies.append(copy)

    def whiten(p):
        first, last = panel_rows * p, panel_rows * (p + 1)
        rows = lax.broadcasted_iota(jnp.int32, (panel_rows, order), 0) + first
        columns = lax.broadcasted_iota(jnp.int32, (panel_rows, order), 1)
        factor[first:last, :] = jnp.where(columns >= rows, work[first:last, :order], 0.0)
        inverse = jnp.where(columns <= rows, work[first:last, half : half + order], 0.0)
        upper, lower = split(inverse, 2)
        far = last - cut
        lines = [slice(2 * rest, 2 * rest + cut), slice(2 * rest + cut, 2 * order)]
        tops = [upper[:, :cut], upper[:, :cut]]
        bottoms = [lower[:, :cut], jnp.zeros((panel_rows, cut), jnp.bfloat16)]
        if far > 0:
            lines = [slice(0, far), slice(rest, rest + far)] + lines
            tops = [upper[:, cut:last], upper[:, cut:last]] + tops
            bottoms = [lower[:, cut:last], jnp.zeros((panel_rows, far), jnp.bfloat16)] + bottoms
        left = jnp.concatenate(
            [jnp.concatenate(tops, axis=1), jnp.concatenate(bottoms, axis=1)], axis=0
        )

        def step(g):
            lanes = slice(256 * g, 256 * g + 256)
            right = jnp.concatenate([feature_ref[part, lanes] for part in lines], axis=0)
            both = jnp.dot(left, right, preferred_element_type=jnp.float32)
            solved = both[:panel_rows] + both[panel_rows:]
            for k in range(2):
                place = first * tiles + 2 * g + k
                spread[pl.ds(place, panel_rows, stride=tiles), :] = solved[:, 128 * k : 128 * k + 128]
            if g == tiles // 2 - 1:
                values = spread[first * tiles : last * tiles, :]
                shape = (1, panel_rows) + white.shape[2:]
                white[:, first:last] = values.reshape(shape).astype(white.dtype)
                store(p)

        return step

    def nothing(g):
        pass

    if begun:
        work[:panel_rows, :] = top_ref[...]
        load_tail(tail_ref, work)
        regularise(work, panel_rows, order, cells_total)
    else:
        load_packed(packed_ref, work, order)
        regularise(work, 0, order, cells_total)
        eliminate_panel(work, 0, nothing)
    panels = order // panel_rows
    for p in range(1, panels):
        update_below(work, panel_rows * (p - 1), order)
        eliminate_panel(work, panel_rows * p, whiten(p - 1))
    step = whiten(panels - 1)
    for g in range(tiles // 2):
        step(g)
    for copy in copies:
        copy.wait()


def plane_device(place, subs):
    return {"slab": lax.div(place, subs), "sub": lax.rem(place, subs)}


def store_features(feature_ref, values, lanes):
    cut, rest = feature_cut, values.shape[0] - feature_cut
    upper, lower = split(values, 2)
    feature_ref[:rest, lanes] = upper[cut:]
    feature_ref[rest : 2 * rest, lanes] = lower[cut:]
    feature_ref[2 * rest : 2 * rest + cut, lanes] = upper[:cut]
    feature_ref[2 * rest + cut :, lanes] = lower[:cut]


def pair(center, ahead_one, behind_one, ahead_two, behind_two):
    first = 8.0 * (ahead_one - behind_one) - (ahead_two - behind_two)
    second = 16.0 * (ahead_one + behind_one) - (ahead_two + behind_two) - 30.0 * center
    return first * (1.0 / 12.0), second * (1.0 / 12.0)


def selection(features, terms_ref, mix_ref):
    square_rows = lax.broadcasted_iota(jnp.int32, (features, features), 0)
    square_columns = lax.broadcasted_iota(jnp.int32, (features, features), 1)

    def upright(row):
        return jnp.sum(jnp.where(square_rows == square_columns, row, 0.0), axis=1, keepdims=True)

    slot = lax.broadcasted_iota(jnp.int32, (features, 256), 1)
    base_of = lax.rem(slot, 32).astype(jnp.float32)
    left, middle, right = [
        (upright(terms_ref[k : k + 1, :].astype(jnp.float32)) == base_of).astype(jnp.float32)
        for k in range(3)
    ]
    first, second, third = [part.astype(jnp.float32) for part in split(upright(mix_ref[...]), 3)]
    weights = jnp.where(slot < 96, first, jnp.where(slot < 192, second, third))
    left = jnp.where(slot < 96, left, 0.0)
    middle = jnp.where(slot < 96, middle, 0.0)
    right = jnp.where(slot < 224, right * weights, 0.0)
    return jnp.concatenate([left, middle + right], axis=0).astype(jnp.bfloat16)


def picked_products(natural, start, choose, scale):
    features = choose.shape[0] // 2
    cells_rows = natural.shape[0] // 32
    pieces = []
    for at in (start, start + 1):
        parts = split(natural[pl.ds(at, 32, stride=cells_rows), :], 3)
        pieces.append(jnp.concatenate(parts + parts + [parts[0], parts[0]], axis=0))
    picked = jnp.dot(
        choose, jnp.concatenate(pieces, axis=1), preferred_element_type=jnp.float32
    )
    return scale * picked[:features] * picked[features:]


def products(left, right):
    return lax.dot_general(
        left, right, (((1,), (1,)), ((), ())), preferred_element_type=jnp.float32
    )


def twin_kernel(
    snaps,
    cells_total,
    fields_in,
    ids_in,
    weight_in,
    terms_in,
    mix_in,
    top_ref,
    tail_ref,
    feature_ref,
    blocks,
    ids_ref,
    weight_ref,
    terms_ref,
    mix_ref,
    load_done,
    other_feature,
    natural,
    other_natural,
    partial,
    landed,
    snaps_sum,
    total,
    halo_send,
    halo_recv,
    core_send,
    core_recv,
    snap_send,
    snap_recv,
    gather_send,
    gather_recv,
):
    slab, sub, snap = lax.axis_index("slab"), lax.axis_index("sub"), lax.axis_index("snap")
    twin = {"sub": 1 - sub}
    across = {"slab": 1 - slab}
    corner = {"slab": 1 - slab, "sub": 1 - sub}
    snap_peers = [{"snap": lax.rem(snap + k, snaps)} for k in range(1, snaps)]
    passed = [lax.convert_element_type(snap <= k, jnp.int32) for k in range(snaps - 1)]
    barrier = pltpu.get_barrier_semaphore()
    for peer in [across, corner, twin] + snap_peers:
        pl.semaphore_signal(barrier, inc=1, device_id=peer, device_id_type=MESH)
    loads = [
        pltpu.make_async_copy(source, target, load_done.at[k])
        for k, (source, target) in enumerate(
            (
                (fields_in, blocks.at[pl.ds(0, 1)]),
                (terms_in, terms_ref),
                (mix_in, mix_ref),
                (weight_in, weight_ref),
                (ids_in, ids_ref),
            )
        )
    ]
    for load in loads:
        load.start()
    loads[0].wait()
    pl.semaphore_wait(barrier, 3 + len(snap_peers))
    halos = []
    for slot, peer in ((1, across), (3, corner), (2, twin)):
        copy = pltpu.make_async_remote_copy(
            src_ref=blocks.at[0],
            dst_ref=blocks.at[slot],
            send_sem=halo_send.at[slot - 1],
            recv_sem=halo_recv.at[slot - 1],
            device_id=peer,
            device_id_type=MESH,
        )
        copy.start()
        halos.append(copy)
    for load in loads[1:]:
        load.wait()
    features = terms_ref.shape[1]
    field_count, layers, columns, width = blocks.shape[1:]
    cells_rows = layers * columns
    choose = selection(features, terms_ref, mix_ref)
    table = lax.broadcasted_iota(jnp.int32, weight_ref.shape, 1)
    scale = jnp.sum(
        jnp.where(table == ids_ref[...], weight_ref[...], 0.0), axis=1, keepdims=True
    )
    line = lax.broadcasted_iota(jnp.int32, (columns, width), 0)

    def put(target, field, kind, layer, tile):
        start = (field * 7 + kind) * cells_rows + layer * columns
        target[start : start + columns, :] = tile

    def along_y(target, block):
        target[28 * cells_rows :, :] = jnp.zeros((4 * cells_rows, width), jnp.float32)
        for f in range(field_count):
            for z in range(layers):
                tile = blocks[block, f, z]
                put(target, f, 0, z, tile)
                first, second = pair(tile, *[pltpu.roll(tile, s % width, 1) for s in (-1, 1, -2, 2)])
                put(target, f, 3, z, first)
                put(target, f, 6, z, second)

    def along_x(target, block, beside):
        for f in range(field_count):
            for z in range(layers):
                tile, other = blocks[block, f, z], blocks[beside, f, z]
                shifts = []
                for s in (-1, 1, -2, 2):
                    inside = line < columns + s if s < 0 else line >= s
                    shifts.append(
                        jnp.where(
                            inside,
                            pltpu.roll(tile, s % columns, 0),
                            pltpu.roll(other, s % columns, 0),
                        )
                    )
                first, second = pair(tile, *shifts)
                put(target, f, 2, z, first)
                put(target, f, 5, z, second)

    def along_z(target, block, beside):
        for f in range(field_count):
            column = [blocks[beside, f, z] for z in range(layers)]
            column = column + [blocks[block, f, z] for z in range(layers)] + column
            for z in range(layers):
                at = layers + z
                first, second = pair(
                    column[at], column[at + 1], column[at - 1], column[at + 2], column[at - 2]
                )
                put(target, f, 1, z, first)
                put(target, f, 4, z, second)

    along_y(natural, 0)
    halos[2].wait()
    along_x(natural, 0, 2)
    halos[0].wait()
    along_z(natural, 0, 1)
    for start in range(0, cells_rows, 2):
        values = picked_products(natural, start, choose, scale)
        store_features(feature_ref, values, slice(start * width, (start + 2) * width))
    along_y(other_natural, 1)
    along_z(other_natural, 1, 0)
    halos[1].wait()
    along_x(other_natural, 1, 3)
    for start in range(0, cells_rows, 2):
        values = picked_products(other_natural, start, choose, scale)
        store_features(other_feature, values, slice(start * width, (start + 2) * width))

    cut, rest = feature_cut, features - feature_cut

    def folded(left, right):
        parts = []
        for values in (feature_ref, other_feature):
            both = products(values[left, :], values[right, :])
            high, low = both.shape[0] // 2, both.shape[1] // 2
            both = both[:high] + both[high:]
            parts.append(both[:, :low] + both[:, low:])
        return parts[0] + parts[1]

    def narrow(square):
        return jnp.concatenate([square[:32], square[32:]], axis=1)

    def place(chunk, lines):
        rows = lines.shape[0] // 2
        partial[chunk, 0] = lines[:rows]
        partial[chunk, 1] = lines[rows:]

    def to_twin(chunk):
        copy = pltpu.make_async_remote_copy(
            src_ref=partial.at[chunk, 1 - sub],
            dst_ref=landed.at[chunk],
            send_sem=core_send.at[chunk],
            recv_sem=core_recv.at[chunk],
            device_id=twin,
            device_id_type=MESH,
        )
        copy.start()
        return copy

    def to_snaps(chunk):
        copies = []
        for k in range(snaps - 1):
            copy = pltpu.make_async_remote_copy(
                src_ref=snaps_sum.at[chunk, snap],
                dst_ref=snaps_sum.at[chunk, snap],
                send_sem=snap_send.at[chunk, k],
                recv_sem=snap_recv.at[chunk, lax.rem(snap + snaps - 1 - (k + passed[k]), snaps)],
                device_id={"snap": k + passed[k]},
                device_id_type=MESH,
            )
            copy.start()
            copies.append(copy)
        return copies

    def to_both(chunk):
        copy = pltpu.make_async_remote_copy(
            src_ref=total.at[chunk, sub],
            dst_ref=total.at[chunk, sub],
            send_sem=gather_send.at[chunk],
            recv_sem=gather_recv.at[chunk],
            device_id=twin,
            device_id_type=MESH,
        )
        copy.start()
        return copy

    last, first = slice(0, 2 * rest), slice(2 * rest, 2 * features)
    side = folded(first, last)
    square = folded(first, first)
    head = jnp.concatenate([square, side[:, :cut]], axis=1)
    place(0, jnp.concatenate([head, narrow(side[:, cut:])], axis=0))
    twins = [to_twin(0)]
    square = folded(last, last)
    place(1, jnp.concatenate([square[:cut], narrow(square[cut:, cut:])], axis=0))
    twins.append(to_twin(1))
    spread = []
    for chunk in range(2):
        twins[chunk].wait()
        snaps_sum[chunk, snap] = partial[chunk, sub] + landed[chunk]
        spread.append(to_snaps(chunk))
    gathers = []

    def gather(chunk):
        for copy in spread[chunk]:
            copy.wait()
        block = snaps_sum[chunk, 0]
        for k in range(1, snaps):
            block = block + snaps_sum[chunk, k]
        total[chunk, sub] = block
        gathers.append(to_both(chunk))

    def beside(g):
        if g == beside_group:
            gather(1)

    gather(0)
    gathers[0].wait()
    load_head(total[0].reshape(96, 128), top_ref)
    regularise(top_ref, 0, panel_rows, cells_total)
    eliminate_panel(top_ref, 0, beside)
    gathers[1].wait()
    tail_ref[...] = total[1].reshape(96, 128)


def gram_kernel(
    counts,
    fields_in,
    ids_in,
    weight_in,
    terms_in,
    mix_in,
    packed_ref,
    feature_out,
    fields_ref,
    ids_ref,
    weight_ref,
    terms_ref,
    mix_ref,
    load_done,
    feature_ref,
    gram_wide,
    halo_z,
    halo_x,
    natural,
    partial,
    landed,
    snaps_sum,
    total,
    halo_send,
    halo_recv,
    plane_send,
    plane_recv,
    snap_send,
    snap_recv,
    gather_send,
    gather_recv,
):
    slabs, subs, snaps = counts
    plane = slabs * subs
    slab, sub, snap = lax.axis_index("slab"), lax.axis_index("sub"), lax.axis_index("snap")
    me = slab * subs + sub
    plane_peers = [plane_device(lax.rem(me + k, plane), subs) for k in range(1, plane)]
    snap_peers = [{"snap": lax.rem(snap + k, snaps)} for k in range(1, snaps)]

    loads = [
        pltpu.make_async_copy(source, target, load_done.at[k])
        for k, (source, target) in enumerate(
            (
                (fields_in, fields_ref),
                (terms_in, terms_ref),
                (mix_in, mix_ref),
                (weight_in, weight_ref),
                (ids_in, ids_ref),
            )
        )
    ]
    for load in loads:
        load.start()
    barrier = pltpu.get_barrier_semaphore()
    for peer in plane_peers + snap_peers:
        pl.semaphore_signal(barrier, inc=1, device_id=peer, device_id_type=MESH)
    for load in loads:
        load.wait()
    features = terms_ref.shape[1]
    field_count, layers, columns, width = fields_ref.shape[1:]
    cells_rows = layers * columns
    choose = selection(features, terms_ref, mix_ref)
    table = lax.broadcasted_iota(jnp.int32, weight_ref.shape, 1)
    scale = jnp.sum(
        jnp.where(table == ids_ref[...], weight_ref[...], 0.0), axis=1, keepdims=True
    )
    natural[28 * cells_rows :, :] = jnp.zeros((4 * cells_rows, width), jnp.float32)

    def put(field, kind, layer, tile):
        start = (field * 7 + kind) * cells_rows + layer * columns
        natural[start : start + columns, :] = tile

    for f in range(field_count):
        for z in range(layers):
            tile = fields_ref[0, f, z]
            put(f, 0, z, tile)
            y_shifts = [pltpu.roll(tile, s % width, 1) for s in (-1, 1, -2, 2)]
            first, second = pair(tile, *y_shifts)
            put(f, 3, z, first)
            put(f, 6, z, second)

    pl.semaphore_wait(barrier, len(plane_peers) + len(snap_peers))

    copies = []
    for axis, index, count, halo, base in (
        ("slab", slab, slabs, halo_z, 0),
        ("sub", sub, subs, halo_x, 2),
    ):
        for side, move in ((0, 1), (1, count - 1))[: 1 if count == 2 else 2]:
            copy = pltpu.make_async_remote_copy(
                src_ref=fields_ref.at[0],
                dst_ref=halo.at[side],
                send_sem=halo_send.at[base + side],
                recv_sem=halo_recv.at[base + side],
                device_id={axis: lax.rem(index + move, count)},
                device_id_type=MESH,
            )
            copy.start()
            copies.append(copy)

    for copy in copies:
        copy.wait()

    z_low, z_high = 0, 0 if slabs == 2 else 1
    x_low, x_high = 0, 0 if subs == 2 else 1
    line = lax.broadcasted_iota(jnp.int32, (columns, width), 0)
    for f in range(field_count):
        column = [halo_z[z_low, f, z] for z in range(layers)]
        column += [fields_ref[0, f, z] for z in range(layers)]
        column += [halo_z[z_high, f, z] for z in range(layers)]
        for z in range(layers):
            tile = column[layers + z]
            at = layers + z
            first, second = pair(
                tile, column[at + 1], column[at - 1], column[at + 2], column[at - 2]
            )
            put(f, 1, z, first)
            put(f, 4, z, second)
            low, high = halo_x[x_low, f, z], halo_x[x_high, f, z]
            shifts = []
            for s in (-1, 1, -2, 2):
                turned = pltpu.roll(tile, s % columns, 0)
                other = pltpu.roll(high if s < 0 else low, s % columns, 0)
                inside = line < columns + s if s < 0 else line >= s
                shifts.append(jnp.where(inside, turned, other))
            first, second = pair(tile, *shifts)
            put(f, 2, z, first)
            put(f, 5, z, second)

    for start in range(0, cells_rows, 2):
        lanes = slice(start * width, (start + 2) * width)
        values = picked_products(natural, start, choose, scale)
        feature_ref[:, lanes] = values
        store_features(feature_out, values, lanes)

    everything = feature_ref[...]
    wide = gram_wide.shape[1]
    gram_wide[:, :features] = lax.dot_general(
        everything,
        everything,
        (((1,), (1,)), ((), ())),
        precision=HIGHEST,
        preferred_element_type=jnp.float32,
    )
    half = features // 2
    above = gram_wide[:half, :]
    below = gram_wide[half:, :]
    row = lax.broadcasted_iota(jnp.int32, (half, wide), 0)
    lane = lax.broadcasted_iota(jnp.int32, (half, wide), 1)
    corner = jnp.sum(jnp.where(lane == row + half, below, 0.0), axis=1, keepdims=True)
    packed = jnp.where(
        lane < half,
        jnp.where(lane >= row, above, pltpu.roll(below, wide - half, 1)),
        jnp.where(lane < features, above, corner),
    )
    rows = half // plane
    for k in range(plane):
        partial[k] = packed[k * rows : (k + 1) * rows, :]

    copies = []
    for k in range(1, plane):
        copy = pltpu.make_async_remote_copy(
            src_ref=partial.at[lax.rem(me + k, plane)],
            dst_ref=landed.at[k - 1],
            send_sem=plane_send.at[k - 1],
            recv_sem=plane_recv.at[k - 1],
            device_id=plane_peers[k - 1],
            device_id_type=MESH,
        )
        copy.start()
        copies.append(copy)
    block = partial[me]
    for k in range(1, plane):
        copies[k - 1].wait()
        block = block + landed[k - 1]
    snaps_sum[snap] = block

    copies = []
    for k in range(1, snaps):
        copy = pltpu.make_async_remote_copy(
            src_ref=snaps_sum.at[snap],
            dst_ref=snaps_sum.at[snap],
            send_sem=snap_send.at[k - 1],
            recv_sem=snap_recv.at[k - 1],
            device_id=snap_peers[k - 1],
            device_id_type=MESH,
        )
        copy.start()
        copies.append(copy)
    for copy in copies:
        copy.wait()
    block = snaps_sum[0]
    for k in range(1, snaps):
        block = block + snaps_sum[k]
    total[me] = block

    copies = []
    for k in range(1, plane):
        copy = pltpu.make_async_remote_copy(
            src_ref=total.at[me],
            dst_ref=total.at[me],
            send_sem=gather_send.at[k - 1],
            recv_sem=gather_recv.at[k - 1],
            device_id=plane_peers[k - 1],
            device_id_type=MESH,
        )
        copy.start()
        copies.append(copy)
    for copy in copies:
        copy.wait()
    for k in range(plane):
        packed_ref[k * rows : (k + 1) * rows, :] = total[k]


def local(fields, snap_ids, snap_weight, product_terms, mix_weight):
    counts = tuple(lax.axis_size(axis) for axis in ("slab", "sub", "snap"))
    slabs, subs, snaps = counts
    plane = slabs * subs
    field_count, layers, columns, width = fields.shape[1:]
    features = product_terms.shape[0]
    cells = layers * columns * width
    cells_total = float(snaps * plane * cells)
    half = features // 2
    rows = half // plane
    wide = features // 128 * 128 + 128
    f32 = jnp.float32
    in_vmem = pl.BlockSpec(memory_space=pltpu.VMEM)
    in_hbm = pl.BlockSpec(memory_space=pltpu.HBM)
    dma = pltpu.SemaphoreType.DMA
    operands = (
        fields,
        snap_ids.reshape(1, 1),
        snap_weight.reshape(1, -1),
        product_terms.T,
        mix_weight.reshape(1, -1),
    )
    tables = [
        pltpu.VMEM((1, 1), jnp.int32),
        pltpu.VMEM((1, snap_weight.shape[0]), f32),
        pltpu.VMEM((3, features), jnp.int32),
        pltpu.VMEM((1, features), f32),
        dma((5,)),
    ]
    pairs = pltpu.VMEM((2 * features, cells), jnp.bfloat16)
    bases = pltpu.VMEM((32 * layers * columns, width), f32)
    if (slabs, subs, features) == (2, 2, 3 * feature_cut):
        part = pltpu.VMEM((2, 2, 48, 128), f32)
        results = pl.pallas_call(
            functools.partial(twin_kernel, snaps, cells_total),
            out_shape=(pltpu.VMEM((panel_rows, 2 * wide), f32), pltpu.VMEM((96, 128), f32), pairs),
            in_specs=[in_hbm] * 5,
            out_specs=(in_vmem,) * 3,
            scratch_shapes=[pltpu.VMEM((4,) + fields.shape[1:], f32)]
            + tables
            + [
                pairs,
                bases,
                bases,
                part,
                pltpu.VMEM((2, 48, 128), f32),
                pltpu.VMEM((2, snaps, 48, 128), f32),
                part,
                dma((3,)),
                dma((3,)),
                dma((2,)),
                dma((2,)),
                dma((2, snaps - 1)),
                dma((2, snaps - 1)),
                dma((2,)),
                dma((2,)),
            ],
            compiler_params=pltpu.CompilerParams(collective_id=0, has_side_effects=True),
        )(*operands)
    else:
        results = pl.pallas_call(
            functools.partial(gram_kernel, counts),
            out_shape=(pltpu.VMEM((half, wide), f32), pairs),
            in_specs=[in_hbm] * 5,
            out_specs=(in_vmem, in_vmem),
            scratch_shapes=[pltpu.VMEM(fields.shape, f32)]
            + tables
            + [
                pltpu.VMEM((features, cells), f32),
                pltpu.VMEM((features, wide), f32),
                pltpu.VMEM((2,) + fields.shape[1:], f32),
                pltpu.VMEM((2,) + fields.shape[1:], f32),
                bases,
                pltpu.VMEM((plane, rows, wide), f32),
                pltpu.VMEM((plane - 1, rows, wide), f32),
                pltpu.VMEM((snaps, rows, wide), f32),
                pltpu.VMEM((plane, rows, wide), f32),
                dma((4,)),
                dma((4,)),
                dma((plane - 1,)),
                dma((plane - 1,)),
                dma((snaps - 1,)),
                dma((snaps - 1,)),
                dma((plane - 1,)),
                dma((plane - 1,)),
            ],
            compiler_params=pltpu.CompilerParams(collective_id=0, has_side_effects=True),
        )(*operands)
    white = (1, features, layers, columns, width)
    return pl.pallas_call(
        functools.partial(whiten_kernel, cells_total, len(results) == 3),
        out_shape=(
            jax.ShapeDtypeStruct(white, jnp.bfloat16),
            jax.ShapeDtypeStruct((features, features), f32),
        ),
        in_specs=[in_vmem] * len(results),
        out_specs=(in_hbm, in_hbm),
        scratch_shapes=[
            pltpu.VMEM((features, 2 * wide), f32),
            pltpu.VMEM((features * (cells // 128), 128), f32),
            pltpu.VMEM(white, jnp.bfloat16),
            pltpu.VMEM((features, features), f32),
            dma((2 * features // panel_rows,)),
        ],
        compiler_params=pltpu.CompilerParams(vmem_limit_bytes=24 * 1024 * 1024),
    )(*[pltpu.with_memory_space_constraint(value, pltpu.VMEM) for value in results])


def solution(mesh):
    return jax.shard_map(
        local,
        mesh=mesh,
        in_specs=(
            P(("groups", "snap"), None, "slab", "sub", None),
            P(("groups", "snap")),
            P(),
            P(),
            P(),
        ),
        out_specs=(P(("groups", "snap"), None, "slab", "sub", None), P("groups", None)),
        check_vma=False,
    )
```

```python
import functools

import jax
import jax.numpy as jnp
from jax import lax
from jax.experimental import pallas as pl
from jax.experimental.pallas import tpu as pltpu
from jax.sharding import PartitionSpec as P

ridge_value = 0.05
panel_rows = 64
feature_cut = 64
beside_group = 1
HIGHEST = lax.Precision.HIGHEST
MESH = pl.DeviceIdType.MESH


def split(values, count):
    parts = []
    for _ in range(count):
        part = values.astype(jnp.bfloat16)
        parts.append(part)
        values = values - part.astype(jnp.float32)
    return parts


def row_of(tile, place):
    return jnp.broadcast_to(tile[place : place + 1, :], tile.shape)


def eliminate_group(groups, first, place):
    line = lax.broadcasted_iota(jnp.int32, (8, 128), 0)
    lane_tile, lane = place // 128, place % 128
    later = range(first, len(groups))
    spread = {
        (r, c): jnp.take_along_axis(
            groups[r][lane_tile], jnp.full((8, 128), lane + c, jnp.int32), axis=1
        ) if r == first else jnp.broadcast_to(groups[r][lane_tile][:, lane + c : lane + c + 1], (8, 128))
        for r in later
        for c in range(8)
    }
    pivots = jnp.ones((8, 128), jnp.float32)
    factors = []
    head = {(j, c): row_of(spread[first, c], j) for c in range(8) for j in range(c + 1)}
    inverses = []
    for j in range(0, 8, 2):
        k = j + 1
        one, cross, two = head[j, j], head[j, k], head[k, k]
        first_inverse = 1.0 / one
        product = one * two - cross * cross
        second_inverse = one * (1.0 / product)
        pivots = jnp.where(line == j, one, pivots)
        pivots = jnp.where(line == k, product * first_inverse, pivots)
        ratio = cross * first_inverse
        for c in range(j + 2, 8):
            head[k, c] = head[k, c] - head[j, c] * ratio
        for c in range(j + 2, 8):
            left, right = head[j, c] * first_inverse, head[k, c] * second_inverse
            for d in range(c, 8):
                head[c, d] = (head[c, d] - left * head[j, d]) - right * head[k, d]
        inverses += [first_inverse, second_inverse]
    for j in range(8):
        inverse = inverses[j]
        scaled = {r: spread[r, j] * inverse for r in later}
        scaled[first] = jnp.where(line > j, scaled[first], 0.0)
        factors.append(scaled)
        for c in range(j + 1, 8):
            for r in later:
                spread[r, c] = spread[r, c] - scaled[r] * head[j, c]
    for t in range(len(groups[first])):
        tile = groups[first][t]
        for j in range(8):
            row = row_of(tile, j)
            if j < 7:
                tile = tile - factors[j][first] * row
            for r in later:
                if r > first:
                    groups[r][t] = groups[r][t] - factors[j][r] * row
        groups[first][t] = tile
    return 1.0 / jnp.sqrt(pivots)


def panel_lanes(work, start):
    half = work.shape[1] // 2
    return start // 128 * 128, half + (start + panel_rows + 127) // 128 * 128


def eliminate_panel(work, start, beside):
    low, high = panel_lanes(work, start)
    stop = start + panel_rows
    groups = [
        [work[r : r + 8, t : t + 128] for t in range(low, high, 128)] for r in range(start, stop, 8)
    ]
    for g in range(panel_rows // 8):
        scale = eliminate_group(groups, g, start + 8 * g - low)
        row = start + 8 * g
        work[row : row + 8, low:high] = jnp.concatenate([tile * scale for tile in groups[g]], axis=1)
        beside(g)


def update_below(work, start, order):
    high = panel_lanes(work, start)[1]
    half = work.shape[1] // 2
    stop = start + panel_rows
    near = stop // 128 * 128
    sides = work[start:stop, near:half].T[stop - near : order - near, :]
    panel = work[start:stop, near:high]
    a, b, c = split(sides, 3)
    d, e, f = split(panel, 3)
    left = jnp.concatenate([a, a, b, b, a, c], axis=1)
    right = jnp.concatenate([d, e, d, e, f, d], axis=0)
    work[stop:order, near:high] = work[stop:order, near:high] - jnp.dot(
        left, right, preferred_element_type=jnp.float32
    )


def regularise(work, first, last, cells_total):
    half = work.shape[1] // 2
    rows = lax.broadcasted_iota(jnp.int32, (last - first, half), 0) + first
    columns = lax.broadcasted_iota(jnp.int32, (last - first, half), 1)
    identity = (rows == columns).astype(jnp.float32)
    work[first:last, half:] = identity
    work[first:last, :half] = work[first:last, :half] * (1.0 / cells_total) + ridge_value * identity


def load_packed(packed_ref, work, order):
    middle = packed_ref.shape[0]
    half = work.shape[1] // 2
    row = lax.broadcasted_iota(jnp.int32, (middle, 128), 0)
    lane = lax.broadcasted_iota(jnp.int32, (middle, 128), 1)
    left = packed_ref[:, :128]
    turned = jnp.concatenate([left, jnp.zeros((128 - middle, 128), jnp.float32)], axis=0).T
    turned = turned[:middle, :]
    work[:middle, :128] = jnp.where((lane >= row) | (lane >= middle), left, turned)
    work[:middle, 128:half] = jnp.where(lane + 128 < order, packed_ref[:, 128:], 0.0)
    corner = packed_ref[:, order : order + 1]
    lower = jnp.where(lane < row, left, jnp.where(lane > row, turned, corner))
    lower = jnp.where(lane < middle, lower, 0.0)
    lower = jnp.concatenate([lower, jnp.zeros((middle, half - 128), jnp.float32)], axis=1)
    work[middle:, :half] = pltpu.roll(lower, middle, 1)


def spare(tile):
    lane = lax.broadcasted_iota(jnp.int32, (32, 128), 1)
    near = jnp.where(lane < 64, tile, 0.0)
    far = pltpu.roll(jnp.where(lane >= 64, tile, 0.0), 64, 1)
    return jnp.concatenate([near, far], axis=0)


def load_head(head, work):
    work[:64, :128] = head[:64]
    work[:64, 128:256] = spare(head[64:])


def load_tail(tail, work):
    middle = jnp.concatenate([tail[:64], jnp.zeros((64, 128), jnp.float32)], axis=1)
    work[64:128, :256] = pltpu.roll(middle, 64, 1)
    work[128:192, :128] = jnp.zeros((64, 128), jnp.float32)
    work[128:192, 128:256] = spare(tail[64:])


def whiten_kernel(cells_total, begun, *refs):
    if begun:
        top_ref, tail_ref, feature_ref, *refs = refs
    else:
        packed_ref, feature_ref, *refs = refs
    white_ref, factor_ref, work, spread, white, factor, done = refs
    order = factor.shape[0]
    half = work.shape[1] // 2
    cells = feature_ref.shape[1]
    tiles = cells // 128
    cut, rest = feature_cut, order - feature_cut
    copies = []

    def store(p):
        rows = slice(panel_rows * p, panel_rows * (p + 1))
        for k, (source, target) in enumerate(
            ((factor.at[rows], factor_ref.at[rows]), (white.at[:, rows], white_ref.at[:, rows]))
        ):
            copy = pltpu.make_async_copy(source, target, done.at[2 * p + k])
            copy.start()
            copies.append(copy)

    def whiten(p):
        first, last = panel_rows * p, panel_rows * (p + 1)
        rows = lax.broadcasted_iota(jnp.int32, (panel_rows, order), 0) + first
        columns = lax.broadcasted_iota(jnp.int32, (panel_rows, order), 1)
        factor[first:last, :] = jnp.where(columns >= rows, work[first:last, :order], 0.0)
        inverse = jnp.where(columns <= rows, work[first:last, half : half + order], 0.0)
        upper, lower = split(inverse, 2)
        far = last - cut
        lines = [slice(2 * rest, 2 * rest + cut), slice(2 * rest + cut, 2 * order)]
        tops = [upper[:, :cut], upper[:, :cut]]
        bottoms = [lower[:, :cut], jnp.zeros((panel_rows, cut), jnp.bfloat16)]
        if far > 0:
            lines = [slice(0, far), slice(rest, rest + far)] + lines
            tops = [upper[:, cut:last], upper[:, cut:last]] + tops
            bottoms = [lower[:, cut:last], jnp.zeros((panel_rows, far), jnp.bfloat16)] + bottoms
        left = jnp.concatenate(
            [jnp.concatenate(tops, axis=1), jnp.concatenate(bottoms, axis=1)], axis=0
        )

        def step(g):
            lanes = slice(256 * g, 256 * g + 256)
            right = jnp.concatenate([feature_ref[part, lanes] for part in lines], axis=0)
            both = jnp.dot(left, right, preferred_element_type=jnp.float32)
            solved = both[:panel_rows] + both[panel_rows:]
            for k in range(2):
                place = first * tiles + 2 * g + k
                spread[pl.ds(place, panel_rows, stride=tiles), :] = solved[:, 128 * k : 128 * k + 128]
            if g == tiles // 2 - 1:
                values = spread[first * tiles : last * tiles, :]
                shape = (1, panel_rows) + white.shape[2:]
                white[:, first:last] = values.reshape(shape).astype(white.dtype)
                store(p)

        return step

    def nothing(g):
        pass

    if begun:
        work[:panel_rows, :] = top_ref[...]
        load_tail(tail_ref, work)
        regularise(work, panel_rows, order, cells_total)
    else:
        load_packed(packed_ref, work, order)
        regularise(work, 0, order, cells_total)
        eliminate_panel(work, 0, nothing)
    panels = order // panel_rows
    for p in range(1, panels):
        update_below(work, panel_rows * (p - 1), order)
        eliminate_panel(work, panel_rows * p, whiten(p - 1))
    step = whiten(panels - 1)
    for g in range(tiles // 2):
        step(g)
    for copy in copies:
        copy.wait()


def plane_device(place, subs):
    return {"slab": lax.div(place, subs), "sub": lax.rem(place, subs)}


def store_features(feature_ref, values, lanes):
    cut, rest = feature_cut, values.shape[0] - feature_cut
    upper, lower = split(values, 2)
    feature_ref[:rest, lanes] = upper[cut:]
    feature_ref[rest : 2 * rest, lanes] = lower[cut:]
    feature_ref[2 * rest : 2 * rest + cut, lanes] = upper[:cut]
    feature_ref[2 * rest + cut :, lanes] = lower[:cut]


def pair(center, ahead_one, behind_one, ahead_two, behind_two):
    first = 8.0 * (ahead_one - behind_one) - (ahead_two - behind_two)
    second = 16.0 * (ahead_one + behind_one) - (ahead_two + behind_two) - 30.0 * center
    return first * (1.0 / 12.0), second * (1.0 / 12.0)


def selection(features, terms_ref, mix_ref):
    square_rows = lax.broadcasted_iota(jnp.int32, (features, features), 0)
    square_columns = lax.broadcasted_iota(jnp.int32, (features, features), 1)

    def upright(row):
        return jnp.sum(jnp.where(square_rows == square_columns, row, 0.0), axis=1, keepdims=True)

    slot = lax.broadcasted_iota(jnp.int32, (features, 256), 1)
    base_of = lax.rem(slot, 32).astype(jnp.float32)
    left, middle, right = [
        (upright(terms_ref[k : k + 1, :].astype(jnp.float32)) == base_of).astype(jnp.float32)
        for k in range(3)
    ]
    first, second, third = [part.astype(jnp.float32) for part in split(upright(mix_ref[...]), 3)]
    weights = jnp.where(slot < 96, first, jnp.where(slot < 192, second, third))
    left = jnp.where(slot < 96, left, 0.0)
    middle = jnp.where(slot < 96, middle, 0.0)
    right = jnp.where(slot < 224, right * weights, 0.0)
    return jnp.concatenate([left, middle + right], axis=0).astype(jnp.bfloat16)


def picked_products(natural, start, choose, scale):
    features = choose.shape[0] // 2
    cells_rows = natural.shape[0] // 32
    pieces = []
    for at in (start, start + 1):
        parts = split(natural[pl.ds(at, 32, stride=cells_rows), :], 3)
        pieces.append(jnp.concatenate(parts + parts + [parts[0], parts[0]], axis=0))
    picked = jnp.dot(
        choose, jnp.concatenate(pieces, axis=1), preferred_element_type=jnp.float32
    )
    return scale * picked[:features] * picked[features:]


def products(left, right):
    return lax.dot_general(
        left, right, (((1,), (1,)), ((), ())), preferred_element_type=jnp.float32
    )


def twin_kernel(
    snaps,
    cells_total,
    fields_in,
    ids_in,
    weight_in,
    terms_in,
    mix_in,
    top_ref,
    tail_ref,
    feature_ref,
    blocks,
    ids_ref,
    weight_ref,
    terms_ref,
    mix_ref,
    load_done,
    other_feature,
    natural,
    other_natural,
    partial,
    landed,
    snaps_sum,
    total,
    halo_send,
    halo_recv,
    core_send,
    core_recv,
    snap_send,
    snap_recv,
    gather_send,
    gather_recv,
):
    slab, sub, snap = lax.axis_index("slab"), lax.axis_index("sub"), lax.axis_index("snap")
    twin = {"sub": 1 - sub}
    across = {"slab": 1 - slab}
    corner = {"slab": 1 - slab, "sub": 1 - sub}
    snap_peers = [{"snap": lax.rem(snap + k, snaps)} for k in range(1, snaps)]
    passed = [lax.convert_element_type(snap <= k, jnp.int32) for k in range(snaps - 1)]
    barrier = pltpu.get_barrier_semaphore()
    for peer in [across, corner, twin] + snap_peers:
        pl.semaphore_signal(barrier, inc=1, device_id=peer, device_id_type=MESH)
    loads = [
        pltpu.make_async_copy(source, target, load_done.at[k])
        for k, (source, target) in enumerate(
            (
                (fields_in, blocks.at[pl.ds(0, 1)]),
                (terms_in, terms_ref),
                (mix_in, mix_ref),
                (weight_in, weight_ref),
                (ids_in, ids_ref),
            )
        )
    ]
    for load in loads:
        load.start()
    loads[0].wait()
    pl.semaphore_wait(barrier, 3 + len(snap_peers))
    halos = []
    for slot, peer in ((1, across), (3, corner), (2, twin)):
        copy = pltpu.make_async_remote_copy(
            src_ref=blocks.at[0],
            dst_ref=blocks.at[slot],
            send_sem=halo_send.at[slot - 1],
            recv_sem=halo_recv.at[slot - 1],
            device_id=peer,
            device_id_type=MESH,
        )
        copy.start()
        halos.append(copy)
    for load in loads[1:]:
        load.wait()
    features = terms_ref.shape[1]
    field_count, layers, columns, width = blocks.shape[1:]
    cells_rows = layers * columns
    choose = selection(features, terms_ref, mix_ref)
    table = lax.broadcasted_iota(jnp.int32, weight_ref.shape, 1)
    scale = jnp.sum(
        jnp.where(table == ids_ref[...], weight_ref[...], 0.0), axis=1, keepdims=True
    )
    line = lax.broadcasted_iota(jnp.int32, (columns, width), 0)

    def put(target, field, kind, layer, tile):
        start = (field * 7 + kind) * cells_rows + layer * columns
        target[start : start + columns, :] = tile

    def along_y(target, block):
        target[28 * cells_rows :, :] = jnp.zeros((4 * cells_rows, width), jnp.float32)
        for f in range(field_count):
            for z in range(layers):
                tile = blocks[block, f, z]
                put(target, f, 0, z, tile)
                first, second = pair(tile, *[pltpu.roll(tile, s % width, 1) for s in (-1, 1, -2, 2)])
                put(target, f, 3, z, first)
                put(target, f, 6, z, second)

    def along_x(target, block, beside):
        for f in range(field_count):
            for z in range(layers):
                tile, other = blocks[block, f, z], blocks[beside, f, z]
                shifts = []
                for s in (-1, 1, -2, 2):
                    inside = line < columns + s if s < 0 else line >= s
                    shifts.append(
                        jnp.where(
                            inside,
                            pltpu.roll(tile, s % columns, 0),
                            pltpu.roll(other, s % columns, 0),
                        )
                    )
                first, second = pair(tile, *shifts)
                put(target, f, 2, z, first)
                put(target, f, 5, z, second)

    def along_z(target, block, beside):
        for f in range(field_count):
            column = [blocks[beside, f, z] for z in range(layers)]
            column = column + [blocks[block, f, z] for z in range(layers)] + column
            for z in range(layers):
                at = layers + z
                first, second = pair(
                    column[at], column[at + 1], column[at - 1], column[at + 2], column[at - 2]
                )
                put(target, f, 1, z, first)
                put(target, f, 4, z, second)

    along_y(natural, 0)
    halos[2].wait()
    along_x(natural, 0, 2)
    halos[0].wait()
    along_z(natural, 0, 1)
    for start in range(0, cells_rows, 2):
        values = picked_products(natural, start, choose, scale)
        store_features(feature_ref, values, slice(start * width, (start + 2) * width))
    along_y(other_natural, 1)
    along_z(other_natural, 1, 0)
    halos[1].wait()
    along_x(other_natural, 1, 3)
    for start in range(0, cells_rows, 2):
        values = picked_products(other_natural, start, choose, scale)
        store_features(other_feature, values, slice(start * width, (start + 2) * width))

    cut, rest = feature_cut, features - feature_cut

    def folded(left, right):
        parts = []
        for values in (feature_ref, other_feature):
            both = products(values[left, :], values[right, :])
            high, low = both.shape[0] // 2, both.shape[1] // 2
            both = both[:high] + both[high:]
            parts.append(both[:, :low] + both[:, low:])
        return parts[0] + parts[1]

    def narrow(square):
        return jnp.concatenate([square[:32], square[32:]], axis=1)

    def place(chunk, lines):
        rows = lines.shape[0] // 2
        partial[chunk, 0] = lines[:rows]
        partial[chunk, 1] = lines[rows:]

    def to_twin(chunk):
        copy = pltpu.make_async_remote_copy(
            src_ref=partial.at[chunk, 1 - sub],
            dst_ref=landed.at[chunk],
            send_sem=core_send.at[chunk],
            recv_sem=core_recv.at[chunk],
            device_id=twin,
            device_id_type=MESH,
        )
        copy.start()
        return copy

    def to_snaps(chunk):
        copies = []
        for k in range(snaps - 1):
            copy = pltpu.make_async_remote_copy(
                src_ref=snaps_sum.at[chunk, snap],
                dst_ref=snaps_sum.at[chunk, snap],
                send_sem=snap_send.at[chunk, k],
                recv_sem=snap_recv.at[chunk, lax.rem(snap + snaps - 1 - (k + passed[k]), snaps)],
                device_id={"snap": k + passed[k]},
                device_id_type=MESH,
            )
            copy.start()
            copies.append(copy)
        return copies

    def to_both(chunk):
        copy = pltpu.make_async_remote_copy(
            src_ref=total.at[chunk, sub],
            dst_ref=total.at[chunk, sub],
            send_sem=gather_send.at[chunk],
            recv_sem=gather_recv.at[chunk],
            device_id=twin,
            device_id_type=MESH,
        )
        copy.start()
        return copy

    last, first = slice(0, 2 * rest), slice(2 * rest, 2 * features)
    side = folded(first, last)
    square = folded(first, first)
    head = jnp.concatenate([square, side[:, :cut]], axis=1)
    place(0, jnp.concatenate([head, narrow(side[:, cut:])], axis=0))
    twins = [to_twin(0)]
    square = folded(last, last)
    place(1, jnp.concatenate([square[:cut], narrow(square[cut:, cut:])], axis=0))
    twins.append(to_twin(1))
    spread = []
    for chunk in range(2):
        twins[chunk].wait_recv()
        snaps_sum[chunk, snap] = partial[chunk, sub] + landed[chunk]
        if chunk:
            for copy in spread[0]:
                copy.wait_send()
        spread.append(to_snaps(chunk))
    gathers = []

    def gather(chunk):
        for copy in spread[chunk]:
            copy.wait_recv()
        block = snaps_sum[chunk, 0]
        for k in range(1, snaps):
            block = block + snaps_sum[chunk, k]
        total[chunk, sub] = block
        gathers.append(to_both(chunk))

    def beside(g):
        if g == beside_group:
            gather(1)

    gather(0)
    gathers[0].wait_recv()
    load_head(total[0].reshape(96, 128), top_ref)
    regularise(top_ref, 0, panel_rows, cells_total)
    eliminate_panel(top_ref, 0, beside)
    gathers[1].wait_recv()
    tail_ref[...] = total[1].reshape(96, 128)
    for copy in twins + spread[1] + gathers:
        copy.wait_send()


def gram_kernel(
    counts,
    fields_in,
    ids_in,
    weight_in,
    terms_in,
    mix_in,
    packed_ref,
    feature_out,
    fields_ref,
    ids_ref,
    weight_ref,
    terms_ref,
    mix_ref,
    load_done,
    feature_ref,
    gram_wide,
    halo_z,
    halo_x,
    natural,
    partial,
    landed,
    snaps_sum,
    total,
    halo_send,
    halo_recv,
    plane_send,
    plane_recv,
    snap_send,
    snap_recv,
    gather_send,
    gather_recv,
):
    slabs, subs, snaps = counts
    plane = slabs * subs
    slab, sub, snap = lax.axis_index("slab"), lax.axis_index("sub"), lax.axis_index("snap")
    me = slab * subs + sub
    plane_peers = [plane_device(lax.rem(me + k, plane), subs) for k in range(1, plane)]
    snap_peers = [{"snap": lax.rem(snap + k, snaps)} for k in range(1, snaps)]

    loads = [
        pltpu.make_async_copy(source, target, load_done.at[k])
        for k, (source, target) in enumerate(
            (
                (fields_in, fields_ref),
                (terms_in, terms_ref),
                (mix_in, mix_ref),
                (weight_in, weight_ref),
                (ids_in, ids_ref),
            )
        )
    ]
    for load in loads:
        load.start()
    barrier = pltpu.get_barrier_semaphore()
    for peer in plane_peers + snap_peers:
        pl.semaphore_signal(barrier, inc=1, device_id=peer, device_id_type=MESH)
    for load in loads:
        load.wait()
    features = terms_ref.shape[1]
    field_count, layers, columns, width = fields_ref.shape[1:]
    cells_rows = layers * columns
    choose = selection(features, terms_ref, mix_ref)
    table = lax.broadcasted_iota(jnp.int32, weight_ref.shape, 1)
    scale = jnp.sum(
        jnp.where(table == ids_ref[...], weight_ref[...], 0.0), axis=1, keepdims=True
    )
    natural[28 * cells_rows :, :] = jnp.zeros((4 * cells_rows, width), jnp.float32)

    def put(field, kind, layer, tile):
        start = (field * 7 + kind) * cells_rows + layer * columns
        natural[start : start + columns, :] = tile

    for f in range(field_count):
        for z in range(layers):
            tile = fields_ref[0, f, z]
            put(f, 0, z, tile)
            y_shifts = [pltpu.roll(tile, s % width, 1) for s in (-1, 1, -2, 2)]
            first, second = pair(tile, *y_shifts)
            put(f, 3, z, first)
            put(f, 6, z, second)

    pl.semaphore_wait(barrier, len(plane_peers) + len(snap_peers))

    copies = []
    for axis, index, count, halo, base in (
        ("slab", slab, slabs, halo_z, 0),
        ("sub", sub, subs, halo_x, 2),
    ):
        for side, move in ((0, 1), (1, count - 1))[: 1 if count == 2 else 2]:
            copy = pltpu.make_async_remote_copy(
                src_ref=fields_ref.at[0],
                dst_ref=halo.at[side],
                send_sem=halo_send.at[base + side],
                recv_sem=halo_recv.at[base + side],
                device_id={axis: lax.rem(index + move, count)},
                device_id_type=MESH,
            )
            copy.start()
            copies.append(copy)

    for copy in copies:
        copy.wait()

    z_low, z_high = 0, 0 if slabs == 2 else 1
    x_low, x_high = 0, 0 if subs == 2 else 1
    line = lax.broadcasted_iota(jnp.int32, (columns, width), 0)
    for f in range(field_count):
        column = [halo_z[z_low, f, z] for z in range(layers)]
        column += [fields_ref[0, f, z] for z in range(layers)]
        column += [halo_z[z_high, f, z] for z in range(layers)]
        for z in range(layers):
            tile = column[layers + z]
            at = layers + z
            first, second = pair(
                tile, column[at + 1], column[at - 1], column[at + 2], column[at - 2]
            )
            put(f, 1, z, first)
            put(f, 4, z, second)
            low, high = halo_x[x_low, f, z], halo_x[x_high, f, z]
            shifts = []
            for s in (-1, 1, -2, 2):
                turned = pltpu.roll(tile, s % columns, 0)
                other = pltpu.roll(high if s < 0 else low, s % columns, 0)
                inside = line < columns + s if s < 0 else line >= s
                shifts.append(jnp.where(inside, turned, other))
            first, second = pair(tile, *shifts)
            put(f, 2, z, first)
            put(f, 5, z, second)

    for start in range(0, cells_rows, 2):
        lanes = slice(start * width, (start + 2) * width)
        values = picked_products(natural, start, choose, scale)
        feature_ref[:, lanes] = values
        store_features(feature_out, values, lanes)

    everything = feature_ref[...]
    wide = gram_wide.shape[1]
    gram_wide[:, :features] = lax.dot_general(
        everything,
        everything,
        (((1,), (1,)), ((), ())),
        precision=HIGHEST,
        preferred_element_type=jnp.float32,
    )
    half = features // 2
    above = gram_wide[:half, :]
    below = gram_wide[half:, :]
    row = lax.broadcasted_iota(jnp.int32, (half, wide), 0)
    lane = lax.broadcasted_iota(jnp.int32, (half, wide), 1)
    corner = jnp.sum(jnp.where(lane == row + half, below, 0.0), axis=1, keepdims=True)
    packed = jnp.where(
        lane < half,
        jnp.where(lane >= row, above, pltpu.roll(below, wide - half, 1)),
        jnp.where(lane < features, above, corner),
    )
    rows = half // plane
    for k in range(plane):
        partial[k] = packed[k * rows : (k + 1) * rows, :]

    copies = []
    for k in range(1, plane):
        copy = pltpu.make_async_remote_copy(
            src_ref=partial.at[lax.rem(me + k, plane)],
            dst_ref=landed.at[k - 1],
            send_sem=plane_send.at[k - 1],
            recv_sem=plane_recv.at[k - 1],
            device_id=plane_peers[k - 1],
            device_id_type=MESH,
        )
        copy.start()
        copies.append(copy)
    block = partial[me]
    for k in range(1, plane):
        copies[k - 1].wait()
        block = block + landed[k - 1]
    snaps_sum[snap] = block

    copies = []
    for k in range(1, snaps):
        copy = pltpu.make_async_remote_copy(
            src_ref=snaps_sum.at[snap],
            dst_ref=snaps_sum.at[snap],
            send_sem=snap_send.at[k - 1],
            recv_sem=snap_recv.at[k - 1],
            device_id=snap_peers[k - 1],
            device_id_type=MESH,
        )
        copy.start()
        copies.append(copy)
    for copy in copies:
        copy.wait()
    block = snaps_sum[0]
    for k in range(1, snaps):
        block = block + snaps_sum[k]
    total[me] = block

    copies = []
    for k in range(1, plane):
        copy = pltpu.make_async_remote_copy(
            src_ref=total.at[me],
            dst_ref=total.at[me],
            send_sem=gather_send.at[k - 1],
            recv_sem=gather_recv.at[k - 1],
            device_id=plane_peers[k - 1],
            device_id_type=MESH,
        )
        copy.start()
        copies.append(copy)
    for copy in copies:
        copy.wait()
    for k in range(plane):
        packed_ref[k * rows : (k + 1) * rows, :] = total[k]


def local(fields, snap_ids, snap_weight, product_terms, mix_weight):
    counts = tuple(lax.axis_size(axis) for axis in ("slab", "sub", "snap"))
    slabs, subs, snaps = counts
    plane = slabs * subs
    field_count, layers, columns, width = fields.shape[1:]
    features = product_terms.shape[0]
    cells = layers * columns * width
    cells_total = float(snaps * plane * cells)
    half = features // 2
    rows = half // plane
    wide = features // 128 * 128 + 128
    f32 = jnp.float32
    in_vmem = pl.BlockSpec(memory_space=pltpu.VMEM)
    in_hbm = pl.BlockSpec(memory_space=pltpu.HBM)
    dma = pltpu.SemaphoreType.DMA
    operands = (
        fields,
        snap_ids.reshape(1, 1),
        snap_weight.reshape(1, -1),
        product_terms.T,
        mix_weight.reshape(1, -1),
    )
    tables = [
        pltpu.VMEM((1, 1), jnp.int32),
        pltpu.VMEM((1, snap_weight.shape[0]), f32),
        pltpu.VMEM((3, features), jnp.int32),
        pltpu.VMEM((1, features), f32),
        dma((5,)),
    ]
    pairs = pltpu.VMEM((2 * features, cells), jnp.bfloat16)
    bases = pltpu.VMEM((32 * layers * columns, width), f32)
    if (slabs, subs, features) == (2, 2, 3 * feature_cut):
        part = pltpu.VMEM((2, 2, 48, 128), f32)
        results = pl.pallas_call(
            functools.partial(twin_kernel, snaps, cells_total),
            out_shape=(pltpu.VMEM((panel_rows, 2 * wide), f32), pltpu.VMEM((96, 128), f32), pairs),
            in_specs=[in_hbm] * 5,
            out_specs=(in_vmem,) * 3,
            scratch_shapes=[pltpu.VMEM((4,) + fields.shape[1:], f32)]
            + tables
            + [
                pairs,
                bases,
                bases,
                part,
                pltpu.VMEM((2, 48, 128), f32),
                pltpu.VMEM((2, snaps, 48, 128), f32),
                part,
                dma((3,)),
                dma((3,)),
                dma((2,)),
                dma((2,)),
                dma((2, snaps - 1)),
                dma((2, snaps - 1)),
                dma((2,)),
                dma((2,)),
            ],
            compiler_params=pltpu.CompilerParams(collective_id=0, has_side_effects=True),
        )(*operands)
    else:
        results = pl.pallas_call(
            functools.partial(gram_kernel, counts),
            out_shape=(pltpu.VMEM((half, wide), f32), pairs),
            in_specs=[in_hbm] * 5,
            out_specs=(in_vmem, in_vmem),
            scratch_shapes=[pltpu.VMEM(fields.shape, f32)]
            + tables
            + [
                pltpu.VMEM((features, cells), f32),
                pltpu.VMEM((features, wide), f32),
                pltpu.VMEM((2,) + fields.shape[1:], f32),
                pltpu.VMEM((2,) + fields.shape[1:], f32),
                bases,
                pltpu.VMEM((plane, rows, wide), f32),
                pltpu.VMEM((plane - 1, rows, wide), f32),
                pltpu.VMEM((snaps, rows, wide), f32),
                pltpu.VMEM((plane, rows, wide), f32),
                dma((4,)),
                dma((4,)),
                dma((plane - 1,)),
                dma((plane - 1,)),
                dma((snaps - 1,)),
                dma((snaps - 1,)),
                dma((plane - 1,)),
                dma((plane - 1,)),
            ],
            compiler_params=pltpu.CompilerParams(collective_id=0, has_side_effects=True),
        )(*operands)
    white = (1, features, layers, columns, width)
    return pl.pallas_call(
        functools.partial(whiten_kernel, cells_total, len(results) == 3),
        out_shape=(
            jax.ShapeDtypeStruct(white, jnp.bfloat16),
            jax.ShapeDtypeStruct((features, features), f32),
        ),
        in_specs=[in_vmem] * len(results),
        out_specs=(in_hbm, in_hbm),
        scratch_shapes=[
            pltpu.VMEM((features, 2 * wide), f32),
            pltpu.VMEM((features * (cells // 128), 128), f32),
            pltpu.VMEM(white, jnp.bfloat16),
            pltpu.VMEM((features, features), f32),
            dma((2 * features // panel_rows,)),
        ],
        compiler_params=pltpu.CompilerParams(vmem_limit_bytes=24 * 1024 * 1024),
    )(*[pltpu.with_memory_space_constraint(value, pltpu.VMEM) for value in results])


def solution(mesh):
    return jax.shard_map(
        local,
        mesh=mesh,
        in_specs=(
            P(("groups", "snap"), None, "slab", "sub", None),
            P(("groups", "snap")),
            P(),
            P(),
            P(),
        ),
        out_specs=(P(("groups", "snap"), None, "slab", "sub", None), P("groups", None)),
        check_vma=False,
    )
```

```python
import functools

import jax
import jax.numpy as jnp
from jax import lax
from jax.experimental import pallas as pl
from jax.experimental.pallas import tpu as pltpu
from jax.sharding import PartitionSpec as P

ridge_value = 0.05
panel_rows = 64
feature_cut = 64
beside_group = 1
HIGHEST = lax.Precision.HIGHEST
MESH = pl.DeviceIdType.MESH


def split(values, count):
    parts = []
    for _ in range(count):
        part = values.astype(jnp.bfloat16)
        parts.append(part)
        values = values - part.astype(jnp.float32)
    return parts


def row_of(tile, place):
    return jnp.broadcast_to(tile[place : place + 1, :], tile.shape)


def eliminate_group(groups, first, place):
    line = lax.broadcasted_iota(jnp.int32, (8, 128), 0)
    lane_tile, lane = place // 128, place % 128
    later = range(first, len(groups))
    spread = {
        (r, c): jnp.take_along_axis(
            groups[r][lane_tile], jnp.full((8, 128), lane + c, jnp.int32), axis=1
        ) if r == first else jnp.broadcast_to(groups[r][lane_tile][:, lane + c : lane + c + 1], (8, 128))
        for r in later
        for c in range(8)
    }
    pivots = jnp.ones((8, 128), jnp.float32)
    factors = []
    head = {(j, c): row_of(spread[first, c], j) for c in range(8) for j in range(c + 1)}
    inverses = []
    for j in range(0, 8, 2):
        k = j + 1
        one, cross, two = head[j, j], head[j, k], head[k, k]
        first_inverse = 1.0 / one
        product = one * two - cross * cross
        second_inverse = one * (1.0 / product)
        pivots = jnp.where(line == j, one, pivots)
        pivots = jnp.where(line == k, product * first_inverse, pivots)
        ratio = cross * first_inverse
        for c in range(j + 2, 8):
            head[k, c] = head[k, c] - head[j, c] * ratio
        for c in range(j + 2, 8):
            left, right = head[j, c] * first_inverse, head[k, c] * second_inverse
            for d in range(c, 8):
                head[c, d] = (head[c, d] - left * head[j, d]) - right * head[k, d]
        inverses += [first_inverse, second_inverse]
    for j in range(8):
        inverse = inverses[j]
        scaled = {r: spread[r, j] * inverse for r in later}
        scaled[first] = jnp.where(line > j, scaled[first], 0.0)
        factors.append(scaled)
        for c in range(j + 1, 8):
            for r in later:
                spread[r, c] = spread[r, c] - scaled[r] * head[j, c]
    for t in range(len(groups[first])):
        tile = groups[first][t]
        for j in range(8):
            row = row_of(tile, j)
            if j < 7:
                tile = tile - factors[j][first] * row
            for r in later:
                if r > first:
                    groups[r][t] = groups[r][t] - factors[j][r] * row
        groups[first][t] = tile
    return 1.0 / jnp.sqrt(pivots)


def panel_lanes(work, start):
    order = work.shape[1] // 2
    return start // 128 * 128, (order + start + panel_rows + 127) // 128 * 128


def eliminate_panel(work, start, beside):
    low, high = panel_lanes(work, start)
    stop = start + panel_rows
    groups = [
        [work[r : r + 8, t : t + 128] for t in range(low, high, 128)] for r in range(start, stop, 8)
    ]
    for g in range(panel_rows // 8):
        scale = eliminate_group(groups, g, start + 8 * g - low)
        row = start + 8 * g
        work[row : row + 8, low:high] = jnp.concatenate([tile * scale for tile in groups[g]], axis=1)
        beside(g)


def update_below(work, start, order):
    high = panel_lanes(work, start)[1]
    half = (order + 127) // 128 * 128
    stop = start + panel_rows
    near = stop // 128 * 128
    sides = work[start:stop, near:half].T[stop - near : order - near, :]
    panel = work[start:stop, near:high]
    a, b, c = split(sides, 3)
    d, e, f = split(panel, 3)
    left = jnp.concatenate([a, a, b, b, a, c], axis=1)
    right = jnp.concatenate([d, e, d, e, f, d], axis=0)
    work[stop:order, near:high] = work[stop:order, near:high] - jnp.dot(
        left, right, preferred_element_type=jnp.float32
    )


def regularise(work, first, last, cells_total):
    order = work.shape[1] // 2
    rows = lax.broadcasted_iota(jnp.int32, (last - first, 2 * order), 0) + first
    columns = lax.broadcasted_iota(jnp.int32, (last - first, 2 * order), 1)
    half = (order + 127) // 128 * 128
    inverse = (columns == rows + order).astype(jnp.float32)
    ridge = jnp.where(columns == rows, ridge_value, 0.0)[:, :half]
    gram = work[first:last, :half] * (1.0 / cells_total) + ridge
    work[first:last, :half] = jnp.where(columns[:, :half] < order, gram, inverse[:, :half])
    work[first:last, half:] = inverse[:, half:]


def load_packed(packed_ref, work, order):
    middle, half = packed_ref.shape
    row = lax.broadcasted_iota(jnp.int32, (middle, 128), 0)
    lane = lax.broadcasted_iota(jnp.int32, (middle, 128), 1)
    left = packed_ref[:, :128]
    turned = jnp.concatenate([left, jnp.zeros((128 - middle, 128), jnp.float32)], axis=0).T
    turned = turned[:middle, :]
    work[:middle, :128] = jnp.where((lane >= row) | (lane >= middle), left, turned)
    work[:middle, 128:half] = jnp.where(lane + 128 < order, packed_ref[:, 128:], 0.0)
    corner = packed_ref[:, order : order + 1]
    lower = jnp.where(lane < row, left, jnp.where(lane > row, turned, corner))
    lower = jnp.where(lane < middle, lower, 0.0)
    lower = jnp.concatenate([lower, jnp.zeros((middle, half - 128), jnp.float32)], axis=1)
    work[middle:, :half] = pltpu.roll(lower, middle, 1)


def spare(tile):
    lane = lax.broadcasted_iota(jnp.int32, (32, 128), 1)
    near = jnp.where(lane < 64, tile, 0.0)
    far = pltpu.roll(jnp.where(lane >= 64, tile, 0.0), 64, 1)
    return jnp.concatenate([near, far], axis=0)


def load_head(head, work):
    work[:64, :128] = head[:64]
    work[:64, 128:256] = spare(head[64:])


def load_tail(tail, work):
    middle = jnp.concatenate([tail[:64], jnp.zeros((64, 128), jnp.float32)], axis=1)
    work[64:128, :256] = pltpu.roll(middle, 64, 1)
    work[128:192, :128] = jnp.zeros((64, 128), jnp.float32)
    work[128:192, 128:256] = spare(tail[64:])


def whiten_kernel(cells_total, begun, *refs):
    if begun:
        top_ref, tail_ref, feature_ref, *refs = refs
    else:
        packed_ref, feature_ref, *refs = refs
    white_ref, factor_ref, work, spread, white, factor, done = refs
    order = factor.shape[0]
    near, apart = order // 128 * 128, order % 128
    cells = feature_ref.shape[1]
    tiles = cells // 128
    cut, rest = feature_cut, order - feature_cut
    copies = []

    def store(p):
        rows = slice(panel_rows * p, panel_rows * (p + 1))
        for k, (source, target) in enumerate(
            ((factor.at[rows], factor_ref.at[rows]), (white.at[:, rows], white_ref.at[:, rows]))
        ):
            copy = pltpu.make_async_copy(source, target, done.at[2 * p + k])
            copy.start()
            copies.append(copy)

    def whiten(p):
        first, last = panel_rows * p, panel_rows * (p + 1)
        rows = lax.broadcasted_iota(jnp.int32, (panel_rows, order), 0) + first
        columns = lax.broadcasted_iota(jnp.int32, (panel_rows, order), 1)
        factor[first:last, :] = jnp.where(columns >= rows, work[first:last, :order], 0.0)
        inverse = pltpu.roll(work[first:last, near:], 2 * order - near - apart, 1)[:, :order]
        inverse = jnp.where(columns <= rows, inverse, 0.0)
        upper, lower = split(inverse, 2)
        far = last - cut
        lines = [slice(2 * rest, 2 * rest + cut), slice(2 * rest + cut, 2 * order)]
        tops = [upper[:, :cut], upper[:, :cut]]
        bottoms = [lower[:, :cut], jnp.zeros((panel_rows, cut), jnp.bfloat16)]
        if far > 0:
            lines = [slice(0, far), slice(rest, rest + far)] + lines
            tops = [upper[:, cut:last], upper[:, cut:last]] + tops
            bottoms = [lower[:, cut:last], jnp.zeros((panel_rows, far), jnp.bfloat16)] + bottoms
        left = jnp.concatenate(
            [jnp.concatenate(tops, axis=1), jnp.concatenate(bottoms, axis=1)], axis=0
        )

        def step(g):
            lanes = slice(256 * g, 256 * g + 256)
            right = jnp.concatenate([feature_ref[part, lanes] for part in lines], axis=0)
            both = jnp.dot(left, right, preferred_element_type=jnp.float32)
            solved = both[:panel_rows] + both[panel_rows:]
            for k in range(2):
                place = first * tiles + 2 * g + k
                spread[pl.ds(place, panel_rows, stride=tiles), :] = solved[:, 128 * k : 128 * k + 128]
            if g == tiles // 2 - 1:
                values = spread[first * tiles : last * tiles, :]
                shape = (1, panel_rows) + white.shape[2:]
                white[:, first:last] = values.reshape(shape).astype(white.dtype)
                store(p)

        return step

    def nothing(g):
        pass

    if begun:
        work[:panel_rows, :] = top_ref[...]
        load_tail(tail_ref, work)
        regularise(work, panel_rows, order, cells_total)
    else:
        load_packed(packed_ref, work, order)
        regularise(work, 0, order, cells_total)
        eliminate_panel(work, 0, nothing)
    panels = order // panel_rows
    for p in range(1, panels):
        update_below(work, panel_rows * (p - 1), order)
        eliminate_panel(work, panel_rows * p, whiten(p - 1))
    step = whiten(panels - 1)
    for g in range(tiles // 2):
        step(g)
    for copy in copies:
        copy.wait()


def plane_device(place, subs):
    return {"slab": lax.div(place, subs), "sub": lax.rem(place, subs)}


def store_features(feature_ref, values, lanes):
    cut, rest = feature_cut, values.shape[0] - feature_cut
    upper, lower = split(values, 2)
    feature_ref[:rest, lanes] = upper[cut:]
    feature_ref[rest : 2 * rest, lanes] = lower[cut:]
    feature_ref[2 * rest : 2 * rest + cut, lanes] = upper[:cut]
    feature_ref[2 * rest + cut :, lanes] = lower[:cut]


def pair(center, ahead_one, behind_one, ahead_two, behind_two):
    first = 8.0 * (ahead_one - behind_one) - (ahead_two - behind_two)
    second = 16.0 * (ahead_one + behind_one) - (ahead_two + behind_two) - 30.0 * center
    return first * (1.0 / 12.0), second * (1.0 / 12.0)


def selection(features, terms_ref, mix_ref):
    square_rows = lax.broadcasted_iota(jnp.int32, (features, features), 0)
    square_columns = lax.broadcasted_iota(jnp.int32, (features, features), 1)

    def upright(row):
        return jnp.sum(jnp.where(square_rows == square_columns, row, 0.0), axis=1, keepdims=True)

    slot = lax.broadcasted_iota(jnp.int32, (features, 256), 1)
    base_of = lax.rem(slot, 32).astype(jnp.float32)
    left, middle, right = [
        (upright(terms_ref[k : k + 1, :].astype(jnp.float32)) == base_of).astype(jnp.float32)
        for k in range(3)
    ]
    first, second, third = [part.astype(jnp.float32) for part in split(upright(mix_ref[...]), 3)]
    weights = jnp.where(slot < 96, first, jnp.where(slot < 192, second, third))
    left = jnp.where(slot < 96, left, 0.0)
    middle = jnp.where(slot < 96, middle, 0.0)
    right = jnp.where(slot < 224, right * weights, 0.0)
    return jnp.concatenate([left, middle + right], axis=0).astype(jnp.bfloat16)


def picked_products(natural, start, choose, scale):
    features = choose.shape[0] // 2
    cells_rows = natural.shape[0] // 32
    pieces = []
    for at in (start, start + 1):
        parts = split(natural[pl.ds(at, 32, stride=cells_rows), :], 3)
        pieces.append(jnp.concatenate(parts + parts + [parts[0], parts[0]], axis=0))
    picked = jnp.dot(
        choose, jnp.concatenate(pieces, axis=1), preferred_element_type=jnp.float32
    )
    return scale * picked[:features] * picked[features:]


def products(left, right):
    return lax.dot_general(
        left, right, (((1,), (1,)), ((), ())), preferred_element_type=jnp.float32
    )


def twin_kernel(
    snaps,
    cells_total,
    fields_in,
    ids_in,
    weight_in,
    terms_in,
    mix_in,
    top_ref,
    tail_ref,
    feature_ref,
    blocks,
    ids_ref,
    weight_ref,
    terms_ref,
    mix_ref,
    load_done,
    other_feature,
    natural,
    other_natural,
    partial,
    landed,
    snaps_sum,
    total,
    halo_send,
    halo_recv,
    core_send,
    core_recv,
    snap_send,
    snap_recv,
    gather_send,
    gather_recv,
):
    slab, sub, snap = lax.axis_index("slab"), lax.axis_index("sub"), lax.axis_index("snap")
    twin = {"sub": 1 - sub}
    across = {"slab": 1 - slab}
    corner = {"slab": 1 - slab, "sub": 1 - sub}
    snap_peers = [{"snap": lax.rem(snap + k, snaps)} for k in range(1, snaps)]
    passed = [lax.convert_element_type(snap <= k, jnp.int32) for k in range(snaps - 1)]
    barrier = pltpu.get_barrier_semaphore()
    for peer in [across, corner, twin] + snap_peers:
        pl.semaphore_signal(barrier, inc=1, device_id=peer, device_id_type=MESH)
    loads = [
        pltpu.make_async_copy(source, target, load_done.at[k])
        for k, (source, target) in enumerate(
            (
                (fields_in, blocks.at[pl.ds(0, 1)]),
                (terms_in, terms_ref),
                (mix_in, mix_ref),
                (weight_in, weight_ref),
                (ids_in, ids_ref),
            )
        )
    ]
    for load in loads:
        load.start()
    loads[0].wait()
    pl.semaphore_wait(barrier, 3 + len(snap_peers))
    halos = []
    for slot, peer in ((1, across), (3, corner), (2, twin)):
        copy = pltpu.make_async_remote_copy(
            src_ref=blocks.at[0],
            dst_ref=blocks.at[slot],
            send_sem=halo_send.at[slot - 1],
            recv_sem=halo_recv.at[slot - 1],
            device_id=peer,
            device_id_type=MESH,
        )
        copy.start()
        halos.append(copy)
    for load in loads[1:]:
        load.wait()
    features = terms_ref.shape[1]
    field_count, layers, columns, width = blocks.shape[1:]
    cells_rows = layers * columns
    choose = selection(features, terms_ref, mix_ref)
    table = lax.broadcasted_iota(jnp.int32, weight_ref.shape, 1)
    scale = jnp.sum(
        jnp.where(table == ids_ref[...], weight_ref[...], 0.0), axis=1, keepdims=True
    )
    line = lax.broadcasted_iota(jnp.int32, (columns, width), 0)

    def put(target, field, kind, layer, tile):
        start = (field * 7 + kind) * cells_rows + layer * columns
        target[start : start + columns, :] = tile

    def along_y(target, block):
        target[28 * cells_rows :, :] = jnp.zeros((4 * cells_rows, width), jnp.float32)
        for f in range(field_count):
            for z in range(layers):
                tile = blocks[block, f, z]
                put(target, f, 0, z, tile)
                first, second = pair(tile, *[pltpu.roll(tile, s % width, 1) for s in (-1, 1, -2, 2)])
                put(target, f, 3, z, first)
                put(target, f, 6, z, second)

    def along_x(target, block, beside):
        for f in range(field_count):
            for z in range(layers):
                tile, other = blocks[block, f, z], blocks[beside, f, z]
                shifts = []
                for s in (-1, 1, -2, 2):
                    inside = line < columns + s if s < 0 else line >= s
                    shifts.append(
                        jnp.where(
                            inside,
                            pltpu.roll(tile, s % columns, 0),
                            pltpu.roll(other, s % columns, 0),
                        )
                    )
                first, second = pair(tile, *shifts)
                put(target, f, 2, z, first)
                put(target, f, 5, z, second)

    def along_z(target, block, beside):
        for f in range(field_count):
            column = [blocks[beside, f, z] for z in range(layers)]
            column = column + [blocks[block, f, z] for z in range(layers)] + column
            for z in range(layers):
                at = layers + z
                first, second = pair(
                    column[at], column[at + 1], column[at - 1], column[at + 2], column[at - 2]
                )
                put(target, f, 1, z, first)
                put(target, f, 4, z, second)

    along_y(natural, 0)
    halos[2].wait()
    along_x(natural, 0, 2)
    halos[0].wait()
    along_z(natural, 0, 1)
    for start in range(0, cells_rows, 2):
        values = picked_products(natural, start, choose, scale)
        store_features(feature_ref, values, slice(start * width, (start + 2) * width))
    along_y(other_natural, 1)
    along_z(other_natural, 1, 0)
    halos[1].wait()
    along_x(other_natural, 1, 3)
    for start in range(0, cells_rows, 2):
        values = picked_products(other_natural, start, choose, scale)
        store_features(other_feature, values, slice(start * width, (start + 2) * width))

    cut, rest = feature_cut, features - feature_cut

    def folded(left, right):
        parts = []
        for values in (feature_ref, other_feature):
            both = products(values[left, :], values[right, :])
            high, low = both.shape[0] // 2, both.shape[1] // 2
            both = both[:high] + both[high:]
            parts.append(both[:, :low] + both[:, low:])
        return parts[0] + parts[1]

    def narrow(square):
        return jnp.concatenate([square[:32], square[32:]], axis=1)

    def place(chunk, lines):
        rows = lines.shape[0] // 2
        partial[chunk, 0] = lines[:rows]
        partial[chunk, 1] = lines[rows:]

    def to_twin(chunk):
        copy = pltpu.make_async_remote_copy(
            src_ref=partial.at[chunk, 1 - sub],
            dst_ref=landed.at[chunk],
            send_sem=core_send.at[chunk],
            recv_sem=core_recv.at[chunk],
            device_id=twin,
            device_id_type=MESH,
        )
        copy.start()
        return copy

    def to_snaps(chunk):
        copies = []
        for k in range(snaps - 1):
            copy = pltpu.make_async_remote_copy(
                src_ref=snaps_sum.at[chunk, snap],
                dst_ref=snaps_sum.at[chunk, snap],
                send_sem=snap_send.at[chunk, k],
                recv_sem=snap_recv.at[chunk, lax.rem(snap + snaps - 1 - (k + passed[k]), snaps)],
                device_id={"snap": k + passed[k]},
                device_id_type=MESH,
            )
            copy.start()
            copies.append(copy)
        return copies

    def to_both(chunk):
        copy = pltpu.make_async_remote_copy(
            src_ref=total.at[chunk, sub],
            dst_ref=total.at[chunk, sub],
            send_sem=gather_send.at[chunk],
            recv_sem=gather_recv.at[chunk],
            device_id=twin,
            device_id_type=MESH,
        )
        copy.start()
        return copy

    last, first = slice(0, 2 * rest), slice(2 * rest, 2 * features)
    side = folded(first, last)
    square = folded(first, first)
    head = jnp.concatenate([square, side[:, :cut]], axis=1)
    place(0, jnp.concatenate([head, narrow(side[:, cut:])], axis=0))
    twins = [to_twin(0)]
    square = folded(last, last)
    place(1, jnp.concatenate([square[:cut], narrow(square[cut:, cut:])], axis=0))
    twins.append(to_twin(1))
    spread = []
    for chunk in range(2):
        twins[chunk].wait_recv()
        snaps_sum[chunk, snap] = partial[chunk, sub] + landed[chunk]
        if chunk:
            for copy in spread[0]:
                copy.wait_send()
        spread.append(to_snaps(chunk))
    gathers = []

    def gather(chunk):
        for copy in spread[chunk]:
            copy.wait_recv()
        block = snaps_sum[chunk, 0]
        for k in range(1, snaps):
            block = block + snaps_sum[chunk, k]
        total[chunk, sub] = block
        gathers.append(to_both(chunk))

    def beside(g):
        if g == beside_group:
            gather(1)

    gather(0)
    gathers[0].wait_recv()
    load_head(total[0].reshape(96, 128), top_ref)
    regularise(top_ref, 0, panel_rows, cells_total)
    eliminate_panel(top_ref, 0, beside)
    gathers[1].wait_recv()
    tail_ref[...] = total[1].reshape(96, 128)
    for copy in twins + spread[1] + gathers:
        copy.wait_send()


def gram_kernel(
    counts,
    fields_in,
    ids_in,
    weight_in,
    terms_in,
    mix_in,
    packed_ref,
    feature_out,
    fields_ref,
    ids_ref,
    weight_ref,
    terms_ref,
    mix_ref,
    load_done,
    feature_ref,
    gram_wide,
    halo_z,
    halo_x,
    natural,
    partial,
    landed,
    snaps_sum,
    total,
    halo_send,
    halo_recv,
    plane_send,
    plane_recv,
    snap_send,
    snap_recv,
    gather_send,
    gather_recv,
):
    slabs, subs, snaps = counts
    plane = slabs * subs
    slab, sub, snap = lax.axis_index("slab"), lax.axis_index("sub"), lax.axis_index("snap")
    me = slab * subs + sub
    plane_peers = [plane_device(lax.rem(me + k, plane), subs) for k in range(1, plane)]
    snap_peers = [{"snap": lax.rem(snap + k, snaps)} for k in range(1, snaps)]

    loads = [
        pltpu.make_async_copy(source, target, load_done.at[k])
        for k, (source, target) in enumerate(
            (
                (fields_in, fields_ref),
                (terms_in, terms_ref),
                (mix_in, mix_ref),
                (weight_in, weight_ref),
                (ids_in, ids_ref),
            )
        )
    ]
    for load in loads:
        load.start()
    barrier = pltpu.get_barrier_semaphore()
    for peer in plane_peers + snap_peers:
        pl.semaphore_signal(barrier, inc=1, device_id=peer, device_id_type=MESH)
    for load in loads:
        load.wait()
    features = terms_ref.shape[1]
    field_count, layers, columns, width = fields_ref.shape[1:]
    cells_rows = layers * columns
    choose = selection(features, terms_ref, mix_ref)
    table = lax.broadcasted_iota(jnp.int32, weight_ref.shape, 1)
    scale = jnp.sum(
        jnp.where(table == ids_ref[...], weight_ref[...], 0.0), axis=1, keepdims=True
    )
    natural[28 * cells_rows :, :] = jnp.zeros((4 * cells_rows, width), jnp.float32)

    def put(field, kind, layer, tile):
        start = (field * 7 + kind) * cells_rows + layer * columns
        natural[start : start + columns, :] = tile

    for f in range(field_count):
        for z in range(layers):
            tile = fields_ref[0, f, z]
            put(f, 0, z, tile)
            y_shifts = [pltpu.roll(tile, s % width, 1) for s in (-1, 1, -2, 2)]
            first, second = pair(tile, *y_shifts)
            put(f, 3, z, first)
            put(f, 6, z, second)

    pl.semaphore_wait(barrier, len(plane_peers) + len(snap_peers))

    copies = []
    for axis, index, count, halo, base in (
        ("slab", slab, slabs, halo_z, 0),
        ("sub", sub, subs, halo_x, 2),
    ):
        for side, move in ((0, 1), (1, count - 1))[: 1 if count == 2 else 2]:
            copy = pltpu.make_async_remote_copy(
                src_ref=fields_ref.at[0],
                dst_ref=halo.at[side],
                send_sem=halo_send.at[base + side],
                recv_sem=halo_recv.at[base + side],
                device_id={axis: lax.rem(index + move, count)},
                device_id_type=MESH,
            )
            copy.start()
            copies.append(copy)

    for copy in copies:
        copy.wait()

    z_low, z_high = 0, 0 if slabs == 2 else 1
    x_low, x_high = 0, 0 if subs == 2 else 1
    line = lax.broadcasted_iota(jnp.int32, (columns, width), 0)
    for f in range(field_count):
        column = [halo_z[z_low, f, z] for z in range(layers)]
        column += [fields_ref[0, f, z] for z in range(layers)]
        column += [halo_z[z_high, f, z] for z in range(layers)]
        for z in range(layers):
            tile = column[layers + z]
            at = layers + z
            first, second = pair(
                tile, column[at + 1], column[at - 1], column[at + 2], column[at - 2]
            )
            put(f, 1, z, first)
            put(f, 4, z, second)
            low, high = halo_x[x_low, f, z], halo_x[x_high, f, z]
            shifts = []
            for s in (-1, 1, -2, 2):
                turned = pltpu.roll(tile, s % columns, 0)
                other = pltpu.roll(high if s < 0 else low, s % columns, 0)
                inside = line < columns + s if s < 0 else line >= s
                shifts.append(jnp.where(inside, turned, other))
            first, second = pair(tile, *shifts)
            put(f, 2, z, first)
            put(f, 5, z, second)

    for start in range(0, cells_rows, 2):
        lanes = slice(start * width, (start + 2) * width)
        values = picked_products(natural, start, choose, scale)
        feature_ref[:, lanes] = values
        store_features(feature_out, values, lanes)

    everything = feature_ref[...]
    wide = gram_wide.shape[1]
    gram_wide[:, :features] = lax.dot_general(
        everything,
        everything,
        (((1,), (1,)), ((), ())),
        precision=HIGHEST,
        preferred_element_type=jnp.float32,
    )
    half = features // 2
    above = gram_wide[:half, :]
    below = gram_wide[half:, :]
    row = lax.broadcasted_iota(jnp.int32, (half, wide), 0)
    lane = lax.broadcasted_iota(jnp.int32, (half, wide), 1)
    corner = jnp.sum(jnp.where(lane == row + half, below, 0.0), axis=1, keepdims=True)
    packed = jnp.where(
        lane < half,
        jnp.where(lane >= row, above, pltpu.roll(below, wide - half, 1)),
        jnp.where(lane < features, above, corner),
    )
    rows = half // plane
    for k in range(plane):
        partial[k] = packed[k * rows : (k + 1) * rows, :]

    copies = []
    for k in range(1, plane):
        copy = pltpu.make_async_remote_copy(
            src_ref=partial.at[lax.rem(me + k, plane)],
            dst_ref=landed.at[k - 1],
            send_sem=plane_send.at[k - 1],
            recv_sem=plane_recv.at[k - 1],
            device_id=plane_peers[k - 1],
            device_id_type=MESH,
        )
        copy.start()
        copies.append(copy)
    block = partial[me]
    for k in range(1, plane):
        copies[k - 1].wait()
        block = block + landed[k - 1]
    snaps_sum[snap] = block

    copies = []
    for k in range(1, snaps):
        copy = pltpu.make_async_remote_copy(
            src_ref=snaps_sum.at[snap],
            dst_ref=snaps_sum.at[snap],
            send_sem=snap_send.at[k - 1],
            recv_sem=snap_recv.at[k - 1],
            device_id=snap_peers[k - 1],
            device_id_type=MESH,
        )
        copy.start()
        copies.append(copy)
    for copy in copies:
        copy.wait()
    block = snaps_sum[0]
    for k in range(1, snaps):
        block = block + snaps_sum[k]
    total[me] = block

    copies = []
    for k in range(1, plane):
        copy = pltpu.make_async_remote_copy(
            src_ref=total.at[me],
            dst_ref=total.at[me],
            send_sem=gather_send.at[k - 1],
            recv_sem=gather_recv.at[k - 1],
            device_id=plane_peers[k - 1],
            device_id_type=MESH,
        )
        copy.start()
        copies.append(copy)
    for copy in copies:
        copy.wait()
    for k in range(plane):
        packed_ref[k * rows : (k + 1) * rows, :] = total[k]


def local(fields, snap_ids, snap_weight, product_terms, mix_weight):
    counts = tuple(lax.axis_size(axis) for axis in ("slab", "sub", "snap"))
    slabs, subs, snaps = counts
    plane = slabs * subs
    field_count, layers, columns, width = fields.shape[1:]
    features = product_terms.shape[0]
    cells = layers * columns * width
    cells_total = float(snaps * plane * cells)
    half = features // 2
    rows = half // plane
    wide = features // 128 * 128 + 128
    f32 = jnp.float32
    in_vmem = pl.BlockSpec(memory_space=pltpu.VMEM)
    in_hbm = pl.BlockSpec(memory_space=pltpu.HBM)
    dma = pltpu.SemaphoreType.DMA
    operands = (
        fields,
        snap_ids.reshape(1, 1),
        snap_weight.reshape(1, -1),
        product_terms.T,
        mix_weight.reshape(1, -1),
    )
    tables = [
        pltpu.VMEM((1, 1), jnp.int32),
        pltpu.VMEM((1, snap_weight.shape[0]), f32),
        pltpu.VMEM((3, features), jnp.int32),
        pltpu.VMEM((1, features), f32),
        dma((5,)),
    ]
    pairs = pltpu.VMEM((2 * features, cells), jnp.bfloat16)
    bases = pltpu.VMEM((32 * layers * columns, width), f32)
    if (slabs, subs, features) == (2, 2, 3 * feature_cut):
        part = pltpu.VMEM((2, 2, 48, 128), f32)
        results = pl.pallas_call(
            functools.partial(twin_kernel, snaps, cells_total),
            out_shape=(pltpu.VMEM((panel_rows, 2 * features), f32), pltpu.VMEM((96, 128), f32), pairs),
            in_specs=[in_hbm] * 5,
            out_specs=(in_vmem,) * 3,
            scratch_shapes=[pltpu.VMEM((4,) + fields.shape[1:], f32)]
            + tables
            + [
                pairs,
                bases,
                bases,
                part,
                pltpu.VMEM((2, 48, 128), f32),
                pltpu.VMEM((2, snaps, 48, 128), f32),
                part,
                dma((3,)),
                dma((3,)),
                dma((2,)),
                dma((2,)),
                dma((2, snaps - 1)),
                dma((2, snaps - 1)),
                dma((2,)),
                dma((2,)),
            ],
            compiler_params=pltpu.CompilerParams(collective_id=0, has_side_effects=True),
        )(*operands)
    else:
        results = pl.pallas_call(
            functools.partial(gram_kernel, counts),
            out_shape=(pltpu.VMEM((half, wide), f32), pairs),
            in_specs=[in_hbm] * 5,
            out_specs=(in_vmem, in_vmem),
            scratch_shapes=[pltpu.VMEM(fields.shape, f32)]
            + tables
            + [
                pltpu.VMEM((features, cells), f32),
                pltpu.VMEM((features, wide), f32),
                pltpu.VMEM((2,) + fields.shape[1:], f32),
                pltpu.VMEM((2,) + fields.shape[1:], f32),
                bases,
                pltpu.VMEM((plane, rows, wide), f32),
                pltpu.VMEM((plane - 1, rows, wide), f32),
                pltpu.VMEM((snaps, rows, wide), f32),
                pltpu.VMEM((plane, rows, wide), f32),
                dma((4,)),
                dma((4,)),
                dma((plane - 1,)),
                dma((plane - 1,)),
                dma((snaps - 1,)),
                dma((snaps - 1,)),
                dma((plane - 1,)),
                dma((plane - 1,)),
            ],
            compiler_params=pltpu.CompilerParams(collective_id=0, has_side_effects=True),
        )(*operands)
    white = (1, features, layers, columns, width)
    return pl.pallas_call(
        functools.partial(whiten_kernel, cells_total, len(results) == 3),
        out_shape=(
            jax.ShapeDtypeStruct(white, jnp.bfloat16),
            jax.ShapeDtypeStruct((features, features), f32),
        ),
        in_specs=[in_vmem] * len(results),
        out_specs=(in_hbm, in_hbm),
        scratch_shapes=[
            pltpu.VMEM((features, 2 * features), f32),
            pltpu.VMEM((features * (cells // 128), 128), f32),
            pltpu.VMEM(white, jnp.bfloat16),
            pltpu.VMEM((features, features), f32),
            dma((2 * features // panel_rows,)),
        ],
        compiler_params=pltpu.CompilerParams(vmem_limit_bytes=24 * 1024 * 1024),
    )(*[pltpu.with_memory_space_constraint(value, pltpu.VMEM) for value in results])


def solution(mesh):
    return jax.shard_map(
        local,
        mesh=mesh,
        in_specs=(
            P(("groups", "snap"), None, "slab", "sub", None),
            P(("groups", "snap")),
            P(),
            P(),
            P(),
        ),
        out_specs=(P(("groups", "snap"), None, "slab", "sub", None), P("groups", None)),
        check_vma=False,
    )
```
